32 devices in a mesh: sect: 2 (over y), seq: 16 (over z, x, core).
Axes of the slice: x: 2, y: 2, z: 4, core: 2. Of those that a mesh axis runs over, the one named last changes fastest.
Arguments:
- qkv: bfloat16 [2, 3, 2048, 5120], P('sect', None, 'seq'), may hold values from -60 to 60
- mask: int32 [2, 16, 16], P('sect'), may hold values from 0 to 1, as said below
- latent: float32 [2, 16, 8192], P('sect', 'seq'), may hold values from -6 to 6
- w_head: bfloat16 [2, 5120, 64], P('sect'), may hold values from -0.078125 to 0.078125
- step: float32 [2], P('sect'), may hold values from -0.9 to -0.3
- dest: int32 [32], replicated, may hold values from 0 to 63, as said below
Outputs:
- next_latents: float32 [2, 32, 8192], P('sect', 'seq')
The draws below stay inside these ranges and needn't reach their ends.
Inputs may be any that keep to these rules, and one draw needn't show every extreme that they name: `mask`: every block may attend itself: the diagonal of each section's block matrix is 1. `dest`: slot numbers are distinct; slot n belongs to device n // 2 in the order sect, then seq; blocks of the second section (indices 16 and up) go to slots 16 * 2 and up.
All inputs are finite; a program needn't handle non-finite values.
Results may differ from the reference program's by a relative error of at most 0.002.
Values may be sent and summed in bfloat16 or wider, within the bound.
A program may use at most 384 MiB of HBM per device.

```python
import jax
import jax.numpy as jnp
from jax import lax

D = 5120
HEADS = 40
HD = 128
LCH = 64
BLK = 128
TOKENS = 2048
NBLK = 16
CAP = 2
N_SEQ = 16


def draw_qkv(key, part):
    k_normal, k_rows, k_cols = jax.random.split(key, 3)
    normal_draw = jnp.clip(jax.random.normal(k_normal, (2, 3, TOKENS, D), jnp.float32), -4.0, 4.0)
    row_scale = jnp.exp(1.1513 * jax.random.uniform(k_rows, (2, TOKENS, 1), jnp.float32))
    rising = jnp.arange(D, dtype=jnp.float32)[None, None, :] / D
    col_scale = jnp.exp(1.0986 * rising + 1.1939 * jax.random.uniform(k_cols, (2, 1, D), jnp.float32))
    queries = normal_draw[:, 0]
    keys_drawn = normal_draw[:, 1]
    value_base = normal_draw[:, 2]
    values = jnp.clip(value_base * row_scale * col_scale, -60.0, 60.0)
    return jnp.stack([queries, keys_drawn, values], axis=1).astype(jnp.bfloat16)


def draw_mask(key, part):
    k_start, k_keep = jax.random.split(key, 2)
    boundary = jax.random.randint(k_start, (2,), 0, max(NBLK // 8, 2)).astype(jnp.int32)
    blocks = jnp.arange(NBLK, dtype=jnp.int32)
    later = blocks[None, :] >= boundary[:, None]
    same_request = later[:, :, None] == later[:, None, :]
    keep_draw = jax.random.randint(k_keep, (2, NBLK, NBLK), 0, 4) > 0
    diagonal = jnp.eye(NBLK, dtype=bool)[None]
    return (same_request & (keep_draw | diagonal)).astype(jnp.int32)


def draw_dest(key, part):
    k_move, k_full, k_rest, k_stay = jax.random.split(key, 4)
    slot_count = N_SEQ * CAP
    moving = jax.random.randint(k_move, (NBLK,), 0, 2).astype(jnp.int32).at[0].set(0)
    full_slots = slot_count - CAP + jax.random.permutation(k_full, CAP).astype(jnp.int32)
    other_slots = jax.random.permutation(k_rest, slot_count - CAP).astype(jnp.int32)
    later_slots = jnp.concatenate([full_slots, other_slots])
    earlier_slots = jnp.concatenate([jnp.zeros((1,), jnp.int32), 1 + jax.random.permutation(k_stay, slot_count - 1).astype(jnp.int32)])
    staying = 1 - moving
    move_rank = jnp.cumsum(moving) - moving
    stay_rank = jnp.cumsum(staying) - staying
    first_dest = jnp.where(moving == 1, slot_count + later_slots[NBLK + move_rank], earlier_slots[stay_rank])
    second_dest = slot_count + later_slots[jnp.arange(NBLK, dtype=jnp.int32)]
    return jnp.concatenate([first_dest, second_dest]).astype(jnp.int32)


def level_of(rng, shape, shards, least, high):
    factor_of, own = 1.0, jax.random.fold_in(rng, 6)
    for dim, parts in shards:
        heights = jnp.exp(jax.random.uniform(jax.random.fold_in(own, dim), (parts,), jnp.float32, least / len(shards), high / len(shards)))
        factor_of = factor_of * jnp.repeat(heights, shape[dim] // parts).reshape([-1 if axis == dim else 1 for axis in range(len(shape))])
    return factor_of


def noise(rng, dims, scale, most, cuts=(), kind=jnp.bfloat16):
    values = jax.random.normal(rng, dims, jnp.float32) * scale
    if len(cuts) > 0:
        values = level_of(rng, dims, cuts, -0.22, 0.18) * values
    return jnp.clip(values, min=-most, max=most).astype(kind)


def setup_inputs(seed: int = 0) -> dict:
    key_list = jax.random.split(jax.random.key(seed), 7)
    qkv = draw_qkv(jax.random.fold_in(key_list[6], 71), 0)
    mask = draw_mask(jax.random.fold_in(key_list[6], 71), 0)
    latent = noise(key_list[2], (2, NBLK, BLK * LCH), 1.0, 6.0, ((0, 2), (1, 16)), jnp.float32)
    w_head = noise(key_list[3], (2, D, LCH), D ** -0.5, 0.078125, ((0, 2),))
    step = jnp.clip(-0.9 + 0.59999996 * jax.random.uniform(key_list[4], (2,), jnp.float32) ** level_of(key_list[4], (2,), ((0, 2),), -0.2, 0.2), -0.9, -0.3)
    dest = draw_dest(jax.random.fold_in(key_list[6], 71), 0)
    return {"qkv": qkv, "mask": mask, "latent": latent, "w_head": w_head, "step": step, "dest": dest}


EPSILON = 1e-06

def attend_section(queries, keys, values, blockmask):
    keys_wide = keys.astype(jnp.float32).reshape(TOKENS, HEADS, HD)
    values_wide = values.astype(jnp.float32).reshape(TOKENS, HEADS, HD)
    score_scale = float(HD) ** (-0.5)

    def one_block(block_index):
        query_rows = lax.dynamic_slice_in_dim(queries, block_index * BLK, BLK, 0)
        query_rows = query_rows.astype(jnp.float32).reshape(BLK, HEADS, HD)
        scores = jnp.einsum('qhd,khd->hqk', query_rows, keys_wide) * score_scale
        mask_row = lax.dynamic_index_in_dim(blockmask, block_index, 0, keepdims=False)
        allowed = jnp.repeat(mask_row > 0, BLK)
        scores = jnp.where(allowed[None, None, :], scores, -jnp.inf)
        row_max = lax.optimization_barrier(jnp.max(scores, axis=2, keepdims=True))
        weights = jnp.exp(scores - row_max)
        denominator = lax.optimization_barrier(jnp.sum(weights, axis=2))
        narrowed = lax.optimization_barrier(weights.astype(jnp.bfloat16))
        widened = narrowed.astype(jnp.float32)
        blended = jnp.einsum('hqk,khd->qhd', widened, values_wide)
        blended = blended / jnp.transpose(denominator)[:, :, None]
        return blended.reshape(BLK, HEADS * HD).astype(jnp.bfloat16)
    blocks = lax.map(one_block, jnp.arange(NBLK, dtype=jnp.int32))
    return blocks.reshape(TOKENS, D)

def reference(qkv, mask, latent, w_head, step, dest):
    placed = []
    for section in range(2):
        attended = attend_section(qkv[section, 0], qkv[section, 1], qkv[section, 2], mask[section])
        mean_square = lax.optimization_barrier(jnp.mean(jnp.square(attended.astype(jnp.float32)), axis=1))
        product = jnp.dot(attended, w_head[section], preferred_element_type=jnp.float32)
        velocity = lax.rsqrt(mean_square + EPSILON)[:, None] * product
        updated = latent[section] + step[section] * velocity.reshape(NBLK, BLK * LCH)
        placed.append(updated)
    all_blocks = jnp.concatenate(placed, axis=0)
    result = jnp.zeros((2 * N_SEQ * CAP, BLK * LCH), jnp.float32).at[dest].set(all_blocks)
    return result.reshape(2, N_SEQ * CAP, BLK * LCH)
```

```python
import functools

import jax
import jax.numpy as jnp
from jax import lax
from jax.experimental import pallas as pl
from jax.experimental.pallas import tpu as pltpu
from jax.sharding import PartitionSpec as P

HD = 128
HG = 8
BLK = 128
CAP = 2


EPSILON = 1e-06


def general_body(qkv, mask, latent, w_head, step, dest):
    groups = lax.axis_size("seq")
    tok_rows = qkv.shape[2]
    features = qkv.shape[3]
    position = lax.axis_index("seq")
    block_count = mask.shape[1]
    score_scale = float(HD) ** (-0.5)
    row_groups = groups // HG
    group_width = features // HG
    per_piece = tok_rows // row_groups
    row_group = position % row_groups
    query_parts = qkv[0, 0].reshape(row_groups, per_piece, HG, group_width)
    pair_parts = qkv[0, 1:].reshape(2, tok_rows, HG, group_width).transpose(2, 0, 1, 3)
    query_send = query_parts.transpose(2, 0, 1, 3).reshape(groups, per_piece, group_width)
    pair_send = jnp.broadcast_to(pair_parts[:, None], (HG, row_groups, 2, tok_rows, group_width))
    pair_send = pair_send.reshape(groups, 2, tok_rows, group_width)
    arrived_query, arrived_pairs = (
        lax.all_to_all(query_send, "seq", split_axis=0, concat_axis=0, tiled=True),
        lax.all_to_all(pair_send, "seq", split_axis=0, concat_axis=0, tiled=True),
    )
    query_rows = arrived_query.reshape(groups * per_piece, group_width)
    key_rows = arrived_pairs[:, 0].reshape(groups * tok_rows, group_width)
    value_rows = arrived_pairs[:, 1].reshape(groups * tok_rows, group_width)
    query_count = groups * per_piece
    query_pos = jnp.arange(groups, dtype=jnp.int32)[:, None] * tok_rows + row_group * per_piece
    query_pos = (query_pos + jnp.arange(per_piece, dtype=jnp.int32)[None, :]).reshape(query_count)
    selector = (
        query_pos[:, None] // BLK == jnp.arange(block_count, dtype=jnp.int32)[None, :]
    ).astype(jnp.bfloat16)
    block_rows = jnp.dot(selector, mask[0].astype(jnp.bfloat16), preferred_element_type=jnp.float32)
    allowed = jnp.broadcast_to((block_rows > 0.5)[:, :, None], (query_count, block_count, BLK))
    allowed = allowed.reshape(query_count, block_count * BLK)
    outputs = []
    for head_index in range(group_width // HD):
        lower = head_index * HD
        scores = (
            jnp.einsum(
                "qd,kd->qk",
                query_rows[:, lower : lower + HD],
                key_rows[:, lower : lower + HD],
                preferred_element_type=jnp.float32,
            )
            * score_scale
        )
        scores = jnp.where(allowed, scores, -jnp.inf)
        row_max = jnp.max(scores, axis=1, keepdims=True)
        weights = jnp.exp(scores - row_max)
        denominator = jnp.sum(weights, axis=1, keepdims=True)
        blended = (
            jnp.dot(
                weights.astype(jnp.bfloat16),
                value_rows[:, lower : lower + HD],
                preferred_element_type=jnp.float32,
            )
            / denominator
        )
        outputs.append(blended.astype(jnp.bfloat16))
    attended = jnp.concatenate(outputs, axis=1)
    homeward = lax.all_to_all(
        attended.reshape(groups, per_piece, group_width),
        "seq",
        split_axis=0,
        concat_axis=0,
        tiled=True,
    )
    token_major = homeward.reshape(HG, row_groups, per_piece, group_width).transpose(1, 2, 0, 3)
    token_major = token_major.reshape(tok_rows, features)
    mean_square = jnp.mean(jnp.square(token_major.astype(jnp.float32)), axis=1)
    product = jnp.dot(token_major, w_head[0], preferred_element_type=jnp.float32)
    velocity = lax.rsqrt(mean_square + EPSILON)[:, None] * product
    updated = latent[0] + step[0] * velocity.reshape(latent.shape[1], latent.shape[2])
    sect_index = lax.axis_index("sect")
    device_rank = sect_index * groups + position
    owned_slots = device_rank * CAP + jnp.arange(CAP, dtype=jnp.int32)
    picker = (owned_slots[:, None] == dest[None, :]).astype(jnp.float32)
    placed = jnp.dot(
        picker,
        lax.all_gather(updated, ("sect", "seq"), axis=0, tiled=True),
        precision=lax.Precision.HIGHEST,
        preferred_element_type=jnp.float32,
    )
    return placed[None]


MESH = pl.DeviceIdType.MESH
LOG2E = 1.4426950408889634
SHARED_BLOCKS = 4
OWN_BLOCKS = 2
UNROLL = 1


def weigh(queries, keys, bias):
    scores = lax.dot_general(
        queries, keys, (((1,), (1,)), ((), ())), preferred_element_type=jnp.float32
    )
    count = bias.shape[0]
    keyed = scores.reshape(count, scores.shape[0] // count, scores.shape[1]) + bias
    scores = keyed.reshape(scores.shape)
    row_max = jnp.max(scores, axis=1, keepdims=True)
    weights = jnp.exp2((scores - row_max) * (LOG2E * float(HD) ** (-0.5)))
    denominator = jnp.sum(weights, axis=1, keepdims=True)
    return weights.astype(jnp.bfloat16), denominator


def blend(weights, denominator, values):
    blended = jnp.dot(weights, values, preferred_element_type=jnp.float32)
    return (blended / denominator).astype(jnp.bfloat16)


def attend(queries, keys, values, bias):
    weights, denominator = weigh(queries, keys, bias)
    return blend(weights, denominator, values)


def kernel(
    groups,
    features,
    qkv,
    mask,
    latent,
    w_head,
    step,
    dest,
    out,
    mask_held,
    latent_held,
    step_held,
    dest_held,
    small_sem,
    w_raw,
    w_own,
    w_sem,
    lat_rows,
    vel_rows,
    sh_q,
    sh_kv,
    own,
    held_weights,
    held_sums,
    bias,
    part,
    sib_part,
    red,
    blocks,
    pick,
    sib_pick,
    send_sem,
    recv_sem,
    local_sem,
    pair_send,
    pair_recv,
    half_send,
    half_recv,
    red_send,
    red_recv,
    blk_send,
    blk_recv,
    swap_send,
    swap_recv,
):
    chips = groups // 2
    pairs = chips // 2
    rows = groups * BLK
    half = BLK // 2
    sect = lax.axis_index("sect")
    me = lax.axis_index("seq")
    chip = me // 2
    core = me % 2
    sibling = chip * 2 + 1 - core

    barrier = pltpu.get_barrier_semaphore()

    def greet_seq(k, _):
        peer = lax.rem(me + k, groups)
        pl.semaphore_signal(barrier, inc=1, device_id=(sect, peer), device_id_type=MESH)
        return 0

    def greet_sect(c, _):
        pl.semaphore_signal(
            barrier, inc=1, device_id=(1 - sect, (c * 2 + chip % 2) * 2 + core), device_id_type=MESH
        )
        return 0

    lax.fori_loop(1, groups, greet_seq, 0)
    lax.fori_loop(0, chips // 2, greet_sect, 0)
    pl.semaphore_wait(barrier, groups - 1 + chips // 2)

    def ends(stage, sender, target):
        t_chip = target // 2
        t_core = target % 2
        if stage < 2:
            columns = pl.ds(pl.multiple_of((t_chip * 5 + 4) * HD, HD), HD)
        else:
            columns = pl.ds(pl.multiple_of((t_chip * 5 + t_core * 2 + min(stage - 2, 1)) * HD, HD), HD)
        place = pl.ds(pl.multiple_of(sender * BLK, BLK), BLK)
        if stage == 0:
            src = qkv.at[0, 0, pl.ds(pl.multiple_of(t_core * half, half), half), columns]
            return src, sh_q.at[sender]
        if stage == 1:
            return qkv.at[0, 1 + t_core, :, columns], sh_kv.at[t_core, place, :]
        if stage == 2:
            return qkv.at[0, :, :, columns], own.at[0, :, place, :]
        if stage == 3:
            return qkv.at[0, pl.ds(0, 2), :, columns], own.at[1, pl.ds(0, 2), place, :]
        return qkv.at[0, 2, :, columns], own.at[1, 2, place, :]

    def remote(stage, sender, target):
        src, dst = ends(stage, sender, target)
        return pltpu.make_async_remote_copy(
            src_ref=src,
            dst_ref=dst,
            send_sem=send_sem.at[stage, target],
            recv_sem=recv_sem.at[stage, sender],
            device_id=(sect, target),
            device_id_type=MESH,
        )

    def local(stage):
        src, dst = ends(stage, me, me)
        return pltpu.make_async_copy(src, dst, local_sem.at[stage])

    def partner(bits):
        found = 0
        place = 1
        while place < groups:
            digit = me // place % 2
            found = found + place * ((1 - digit) if bits & place else digit)
            place *= 2
        return found

    for stages in ((1, 0), (2,), (3,), (4,)):
        for bits in range(1, groups):
            for stage in stages:
                remote(stage, me, partner(bits)).start()
        for stage in stages:
            local(stage).start()

    def arrive(stage):
        def one(k, _):
            sender = lax.rem(me + groups - k, groups)
            src, dst = ends(stage, sender, me)
            pltpu.make_async_remote_copy(
                src_ref=src,
                dst_ref=dst,
                send_sem=send_sem.at[stage, sender],
                recv_sem=recv_sem.at[stage, sender],
                device_id=(sect, sender),
                device_id_type=MESH,
            ).wait_recv()
            return 0

        lax.fori_loop(1, groups, one, 0)
        local(stage).wait()

    w_copies = []
    for slot, head in enumerate((4, core * 2, core * 2 + 1)):
        columns = pl.ds(pl.multiple_of((chip * 5 + head) * HD, HD), HD)
        w_copies.append(
            pltpu.make_async_copy(w_head.at[0, :, columns], w_raw.at[slot], w_sem.at[slot])
        )
        w_copies[-1].start()
    small_copies = [
        pltpu.make_async_copy(mask, mask_held, small_sem.at[0]),
        pltpu.make_async_copy(latent, latent_held, small_sem.at[1]),
        pltpu.make_async_copy(step, step_held, small_sem.at[2]),
        pltpu.make_async_copy(dest, dest_held, small_sem.at[3]),
    ]
    for small in small_copies:
        small.start()
    for small in small_copies:
        small.wait()
    for row in range(half):
        lat_rows[row : row + 1, :] = latent_held[0, :, row * BLK : (row + 1) * BLK]
    for slot in range(3):
        w_copies[slot].wait()
        turned = w_raw[slot]
        w_own[slot, 0] = jnp.concatenate([turned, jnp.zeros_like(turned)], axis=0)
        w_own[slot, 1] = jnp.concatenate([jnp.zeros_like(turned), turned], axis=0)

    expand = (
        lax.broadcasted_iota(jnp.int32, (groups, rows), 1) // BLK
        == lax.broadcasted_iota(jnp.int32, (groups, rows), 0)
    ).astype(jnp.float32)
    wide = jnp.dot(mask_held[0].astype(jnp.float32), expand, preferred_element_type=jnp.float32)
    bias[...] = jnp.where(wide > 0.5, 0.0, -jnp.inf).reshape(groups, 1, rows)

    def pair_copy(index, src, dst):
        return pltpu.make_async_remote_copy(
            src_ref=src,
            dst_ref=dst,
            send_sem=pair_send.at[index],
            recv_sem=pair_recv.at[index],
            device_id=(sect, sibling),
            device_id_type=MESH,
        )

    def contribute(slot, attended, block, first):
        across = (((1,), (1,)), ((), ()))
        product = lax.dot_general(
            attended[:half], w_own[slot, 0], across, preferred_element_type=jnp.float32
        ) + lax.dot_general(
            attended[half:], w_own[slot, 1], across, preferred_element_type=jnp.float32
        )
        wide_out = attended.astype(jnp.float32)
        squared = wide_out * wide_out
        upper = squared.astype(jnp.bfloat16)
        lower = (squared - upper.astype(jnp.float32)).astype(jnp.bfloat16)
        squares = lax.dot_general(
            jnp.ones((8, 2 * HD), jnp.bfloat16),
            jnp.concatenate([upper, lower], axis=1),
            (((1,), (1,)), ((), ())),
            preferred_element_type=jnp.float32,
        )
        both = jnp.concatenate([product, squares], axis=0)
        if first:
            part[block % 2, block // 2] = both
        else:
            part[block % 2, block // 2] += both

    arrive(1)
    handed = pair_copy(0, sh_kv.at[core], sh_kv.at[core])
    handed.start()
    arrive(0)
    pltpu.make_async_remote_copy(
        src_ref=sh_kv.at[1 - core],
        dst_ref=sh_kv.at[1 - core],
        send_sem=pair_send.at[0],
        recv_sem=pair_recv.at[0],
        device_id=(sect, sibling),
        device_id_type=MESH,
    ).wait_recv()

    def shared_step(turn, _):
        first = turn * SHARED_BLOCKS
        queries = sh_q[pl.ds(first, SHARED_BLOCKS)].reshape(SHARED_BLOCKS * half, HD)
        got = attend(queries, sh_kv[0], sh_kv[1], bias[pl.ds(first, SHARED_BLOCKS)])
        got = got.astype(jnp.float32)
        for index in range(SHARED_BLOCKS):
            piece = got[index * half : (index + 1) * half]
            zero = jnp.zeros_like(piece)
            low = jnp.where(core == 0, piece, zero)
            high = jnp.where(core == 0, zero, piece)
            attended = jnp.concatenate([low, high], axis=0).astype(jnp.bfloat16)
            contribute(0, attended, first + index, True)
        return 0

    lax.fori_loop(0, groups // SHARED_BLOCKS, shared_step, 0, unroll=UNROLL)

    for head in range(1):
        arrive(2 + head)

        def own_step(turn, _, head=head):
            first = turn * OWN_BLOCKS
            place = pl.ds(pl.multiple_of(first * BLK, BLK), OWN_BLOCKS * BLK)
            got = attend(
                own[head, 0, place, :], own[head, 1], own[head, 2], bias[pl.ds(first, OWN_BLOCKS)]
            )
            for index in range(OWN_BLOCKS):
                piece = got[index * BLK : (index + 1) * BLK]
                contribute(1 + head, piece, first + index, False)
            return 0

        lax.fori_loop(0, groups // OWN_BLOCKS, own_step, 0, unroll=UNROLL)

    def red_copy(source, target):
        return pltpu.make_async_remote_copy(
            src_ref=part.at[core, target],
            dst_ref=red.at[source],
            send_sem=red_send.at[target],
            recv_sem=red_recv.at[source],
            device_id=(sect, target * 2 + core),
            device_id_type=MESH,
        )

    def half_copy(target):
        return pltpu.make_async_remote_copy(
            src_ref=part.at[1 - core, target],
            dst_ref=sib_part.at[target],
            send_sem=half_send.at[target],
            recv_sem=half_recv.at[target],
            device_id=(sect, sibling),
            device_id_type=MESH,
        )

    def chip_partner(bits):
        found = 0
        place = 1
        while place < chips:
            digit = chip // place % 2
            flip = bits // place % 2
            found = found + place * (digit + flip - 2 * digit * flip)
            place *= 2
        return found

    arrive(3)

    def weigh_step(turn, _):
        first = turn * OWN_BLOCKS
        place = pl.ds(pl.multiple_of(first * BLK, BLK), OWN_BLOCKS * BLK)
        weights, denominator = weigh(own[1, 0, place, :], own[1, 1], bias[pl.ds(first, OWN_BLOCKS)])
        held_weights[place, :] = weights
        held_sums[place, :] = jnp.broadcast_to(denominator, (OWN_BLOCKS * BLK, HD))
        return 0

    lax.fori_loop(0, groups // OWN_BLOCKS, weigh_step, 0)
    arrive(4)

    def join(target):
        half_copy(target).wait_recv()
        part[core, target] += sib_part[target]

    def targets(step):
        turn = step % pairs
        return chip_partner(chips - 1 - 2 * turn), chip_partner(chips - 2 - 2 * turn)

    def settle(step):
        outer, inner = targets(step)
        join(outer)
        red_copy(chip, outer).start()

        @pl.when(step % pairs < pairs - 1)
        def _():
            join(inner)
            red_copy(chip, inner).start()

    def last_step(step, _):
        owner = step // pairs
        outer, inner = targets(step)
        places = [
            pl.ds(pl.multiple_of((target * 2 + owner) * BLK, BLK), BLK) for target in (outer, inner)
        ]
        weights = jnp.concatenate([held_weights[place, :] for place in places], axis=0)
        sums = jnp.concatenate([held_sums[place, :] for place in places], axis=0)
        blended = jnp.dot(weights, own[1, 2], preferred_element_type=jnp.float32)
        got = (blended / sums).astype(jnp.bfloat16)
        contribute(2, got[:BLK], outer * 2 + owner, False)
        contribute(2, got[BLK:], inner * 2 + owner, False)

        @pl.when(owner != core)
        def _():
            half_copy(outer).start()
            half_copy(inner).start()

        @pl.when(jnp.logical_and(step >= 1, (step - 1) // pairs == core))
        def _():
            settle(step - 1)

        return 0

    lax.fori_loop(0, 2 * pairs, last_step, 0)

    @pl.when(core == 1)
    def _():
        settle(2 * pairs - 1)

    join(chip)
    total = part[core, chip]
    for k in range(1, chips):
        source = lax.rem(chip + chips - k, chips)
        red_copy(source, source).wait_recv()
        total = total + red[source]

    levels = chips // 2
    level = chip // 2
    side = chip % 2
    member = me % 4
    scale_row = lax.rsqrt(total[half : half + 1] * (1.0 / features) + EPSILON)
    row_id = lax.broadcasted_iota(jnp.int32, (half, BLK), 0)
    lane_id = lax.broadcasted_iota(jnp.int32, (half, BLK), 1)
    scale_low = jnp.sum(jnp.where(lane_id == row_id, scale_row, 0.0), axis=1, keepdims=True)
    scale_high = jnp.sum(
        jnp.where(lane_id == row_id + half, scale_row, 0.0), axis=1, keepdims=True
    )
    scale = jnp.where(lane_id < half, scale_low, scale_high)
    vel_rows[...] = step_held[0] * (scale * total[:half])
    even = vel_rows[pl.ds(0, half // 2, stride=2), :]
    odd = vel_rows[pl.ds(1, half // 2, stride=2), :]
    upper_rows = jnp.concatenate([even[:, :half], odd[:, :half]], axis=1)
    lower_rows = jnp.concatenate([even[:, half:], odd[:, half:]], axis=1)
    blocks[sect, level] = lat_rows[...] + jnp.concatenate([upper_rows, lower_rows], axis=0)

    def blk_copy(kind, from_sect, source, to_sect, target):
        return pltpu.make_async_remote_copy(
            src_ref=blocks.at[from_sect, source],
            dst_ref=blocks.at[from_sect, source],
            send_sem=blk_send.at[kind, target],
            recv_sem=blk_recv.at[kind, source],
            device_id=(to_sect, (target * 2 + side) * 2 + core),
            device_id_type=MESH,
        )

    @pl.when(sect == 0)
    def _():
        for k in range(levels):
            blk_copy(1, 0, level, 1, lax.rem(level + k, levels)).start()

    for k in range(1, levels):
        blk_copy(0, sect, level, sect, lax.rem(level + k, levels)).start()

    def choose(from_sect, source):
        block = blocks[from_sect, source]
        named = jnp.full(block.shape, dest_held[from_sect * groups + source * 4 + member])
        for owner in range(4):
            for slot in range(CAP):
                number = (sect * groups + level * 4 + owner) * CAP + slot
                pick[owner, slot] += jnp.where(named == number, block, 0.0)

    pick[...] = jnp.zeros_like(pick)
    choose(sect, level)
    for k in range(1, levels):
        source = lax.rem(level + levels - k, levels)
        blk_copy(0, sect, source, sect, source).wait_recv()
        choose(sect, source)

    @pl.when(sect == 1)
    def _():
        for k in range(levels):
            source = lax.rem(level + levels - k, levels)
            blk_copy(1, 0, source, 1, source).wait_recv()
            choose(0, source)

    def swap(source, target):
        return pltpu.make_async_remote_copy(
            src_ref=pick.at[target],
            dst_ref=sib_pick.at[source],
            send_sem=swap_send.at[target],
            recv_sem=swap_recv.at[source],
            device_id=(sect, level * 4 + target),
            device_id_type=MESH,
        )

    for k in (2, 3, 1):
        swap(member, lax.rem(member + k, 4)).start()
    gathered = pick[member]
    for k in (1, 2, 3):
        source = lax.rem(member + 4 - k, 4)
        swap(source, source).wait_recv()
        gathered = gathered + sib_pick[source]
    for slot in range(CAP):
        placed = gathered[slot]
        for row in range(half):
            out[0, slot : slot + 1, row * BLK : (row + 1) * BLK] = placed[row : row + 1]

    half_copy(chip).wait_send()
    handed.wait_send()
    for k in range(1, 4):
        swap(member, lax.rem(member + k, 4)).wait_send()
    for k in range(1, chips):
        target = lax.rem(chip + k, chips)
        red_copy(chip, target).wait_send()
        half_copy(target).wait_send()
    for k in range(1, levels):
        blk_copy(0, sect, level, sect, lax.rem(level + k, levels)).wait_send()

    @pl.when(sect == 0)
    def _():
        for k in range(levels):
            blk_copy(1, 0, level, 1, lax.rem(level + k, levels)).wait_send()

    for stage in range(5):
        def sent(k, _, stage=stage):
            remote(stage, me, lax.rem(me + k, groups)).wait_send()
            return 0

        lax.fori_loop(1, groups, sent, 0)


def kernel_body(qkv, mask, latent, w_head, step, dest):
    groups = lax.axis_size("seq")
    features = qkv.shape[3]
    chips = groups // 2
    rows = groups * BLK
    half = BLK // 2
    channels = w_head.shape[2]
    turned = jnp.swapaxes(w_head, 1, 2)
    vmem = pl.BlockSpec(memory_space=pltpu.VMEM)
    hbm = pl.BlockSpec(memory_space=pl.ANY)
    dma = pltpu.SemaphoreType.DMA
    return pl.pallas_call(
        functools.partial(kernel, groups, features),
        out_shape=jax.ShapeDtypeStruct((1, CAP, latent.shape[2]), jnp.float32),
        in_specs=[hbm, hbm, hbm, hbm, pl.BlockSpec(memory_space=pltpu.HBM), hbm],
        out_specs=vmem,
        scratch_shapes=[
            pltpu.VMEM(mask.shape, jnp.int32),
            pltpu.VMEM(latent.shape, jnp.float32),
            pltpu.SMEM(step.shape, jnp.float32),
            pltpu.SMEM(dest.shape, jnp.int32),
            dma((4,)),
            pltpu.VMEM((3, channels, HD), jnp.bfloat16),
            pltpu.VMEM((3, 2, 2 * channels, HD), jnp.bfloat16),
            dma((3,)),
            pltpu.VMEM((half, BLK), jnp.float32),
            pltpu.VMEM((half, BLK), jnp.float32),
            pltpu.VMEM((groups, half, HD), jnp.bfloat16),
            pltpu.VMEM((2, rows, HD), jnp.bfloat16),
            pltpu.VMEM((2, 3, rows, HD), jnp.bfloat16),
            pltpu.VMEM((rows, rows), jnp.bfloat16),
            pltpu.VMEM((rows, HD), jnp.float32),
            pltpu.VMEM((groups, 1, rows), jnp.float32),
            pltpu.VMEM((2, chips, half + 8, BLK), jnp.float32),
            pltpu.VMEM((chips, half + 8, BLK), jnp.float32),
            pltpu.VMEM((chips, half + 8, BLK), jnp.float32),
            pltpu.VMEM((2, chips // 2, half, BLK), jnp.float32),
            pltpu.VMEM((4, CAP, half, BLK), jnp.float32),
            pltpu.VMEM((4, CAP, half, BLK), jnp.float32),
            dma((5, groups)),
            dma((5, groups)),
            dma((5,)),
            dma((1,)),
            dma((1,)),
            dma((chips,)),
            dma((chips,)),
            dma((chips,)),
            dma((chips,)),
            dma((2, chips // 2)),
            dma((2, chips // 2)),
            dma((4,)),
            dma((4,)),
        ],
        compiler_params=pltpu.CompilerParams(
            collective_id=0, has_side_effects=True, vmem_limit_bytes=61 * 1024 * 1024
        ),
    )(qkv, mask, latent, turned, step, dest)


def body(qkv, mask, latent, w_head, step, dest):
    groups = lax.axis_size("seq")
    heads = qkv.shape[3] // HD
    fits = (
        heads * 2 == groups * 5
        and qkv.shape[2] == BLK
        and latent.shape[1] == 1
        and w_head.shape[2] * 2 == BLK
        and lax.axis_size("sect") == 2
    )
    chosen = kernel_body if fits else general_body
    return chosen(qkv, mask, latent, w_head, step, dest)


def solution(mesh):
    in_specs = (
        P("sect", None, "seq", None),
        P("sect", None, None),
        P("sect", "seq", None),
        P("sect", None, None),
        P("sect"),
        P(),
    )
    out_specs = P("sect", "seq", None)
    return jax.shard_map(body, mesh=mesh, in_specs=in_specs, out_specs=out_specs, check_vma=False)
```

```python
import functools

import jax
import jax.numpy as jnp
from jax import lax
from jax.experimental import pallas as pl
from jax.experimental.pallas import tpu as pltpu
from jax.sharding import PartitionSpec as P

HD = 128
HG = 8
BLK = 128
CAP = 2


EPSILON = 1e-06


def general_body(qkv, mask, latent, w_head, step, dest):
    groups = lax.axis_size("seq")
    tok_rows = qkv.shape[2]
    features = qkv.shape[3]
    position = lax.axis_index("seq")
    block_count = mask.shape[1]
    score_scale = float(HD) ** (-0.5)
    row_groups = groups // HG
    group_width = features // HG
    per_piece = tok_rows // row_groups
    row_group = position % row_groups
    query_parts = qkv[0, 0].reshape(row_groups, per_piece, HG, group_width)
    pair_parts = qkv[0, 1:].reshape(2, tok_rows, HG, group_width).transpose(2, 0, 1, 3)
    query_send = query_parts.transpose(2, 0, 1, 3).reshape(groups, per_piece, group_width)
    pair_send = jnp.broadcast_to(pair_parts[:, None], (HG, row_groups, 2, tok_rows, group_width))
    pair_send = pair_send.reshape(groups, 2, tok_rows, group_width)
    arrived_query, arrived_pairs = (
        lax.all_to_all(query_send, "seq", split_axis=0, concat_axis=0, tiled=True),
        lax.all_to_all(pair_send, "seq", split_axis=0, concat_axis=0, tiled=True),
    )
    query_rows = arrived_query.reshape(groups * per_piece, group_width)
    key_rows = arrived_pairs[:, 0].reshape(groups * tok_rows, group_width)
    value_rows = arrived_pairs[:, 1].reshape(groups * tok_rows, group_width)
    query_count = groups * per_piece
    query_pos = jnp.arange(groups, dtype=jnp.int32)[:, None] * tok_rows + row_group * per_piece
    query_pos = (query_pos + jnp.arange(per_piece, dtype=jnp.int32)[None, :]).reshape(query_count)
    selector = (
        query_pos[:, None] // BLK == jnp.arange(block_count, dtype=jnp.int32)[None, :]
    ).astype(jnp.bfloat16)
    block_rows = jnp.dot(selector, mask[0].astype(jnp.bfloat16), preferred_element_type=jnp.float32)
    allowed = jnp.broadcast_to((block_rows > 0.5)[:, :, None], (query_count, block_count, BLK))
    allowed = allowed.reshape(query_count, block_count * BLK)
    outputs = []
    for head_index in range(group_width // HD):
        lower = head_index * HD
        scores = (
            jnp.einsum(
                "qd,kd->qk",
                query_rows[:, lower : lower + HD],
                key_rows[:, lower : lower + HD],
                preferred_element_type=jnp.float32,
            )
            * score_scale
        )
        scores = jnp.where(allowed, scores, -jnp.inf)
        row_max = jnp.max(scores, axis=1, keepdims=True)
        weights = jnp.exp(scores - row_max)
        denominator = jnp.sum(weights, axis=1, keepdims=True)
        blended = (
            jnp.dot(
                weights.astype(jnp.bfloat16),
                value_rows[:, lower : lower + HD],
                preferred_element_type=jnp.float32,
            )
            / denominator
        )
        outputs.append(blended.astype(jnp.bfloat16))
    attended = jnp.concatenate(outputs, axis=1)
    homeward = lax.all_to_all(
        attended.reshape(groups, per_piece, group_width),
        "seq",
        split_axis=0,
        concat_axis=0,
        tiled=True,
    )
    token_major = homeward.reshape(HG, row_groups, per_piece, group_width).transpose(1, 2, 0, 3)
    token_major = token_major.reshape(tok_rows, features)
    mean_square = jnp.mean(jnp.square(token_major.astype(jnp.float32)), axis=1)
    product = jnp.dot(token_major, w_head[0], preferred_element_type=jnp.float32)
    velocity = lax.rsqrt(mean_square + EPSILON)[:, None] * product
    updated = latent[0] + step[0] * velocity.reshape(latent.shape[1], latent.shape[2])
    sect_index = lax.axis_index("sect")
    device_rank = sect_index * groups + position
    owned_slots = device_rank * CAP + jnp.arange(CAP, dtype=jnp.int32)
    picker = (owned_slots[:, None] == dest[None, :]).astype(jnp.float32)
    placed = jnp.dot(
        picker,
        lax.all_gather(updated, ("sect", "seq"), axis=0, tiled=True),
        precision=lax.Precision.HIGHEST,
        preferred_element_type=jnp.float32,
    )
    return placed[None]


MESH = pl.DeviceIdType.MESH
LOG2E = 1.4426950408889634
SHARED_BLOCKS = 4
OWN_BLOCKS = 2
UNROLL = 1


def weigh(queries, keys, bias):
    scores = lax.dot_general(
        queries, keys, (((1,), (1,)), ((), ())), preferred_element_type=jnp.float32
    )
    count = bias.shape[0]
    keyed = scores.reshape(count, scores.shape[0] // count, scores.shape[1]) + bias
    scores = keyed.reshape(scores.shape)
    row_max = jnp.max(scores, axis=1, keepdims=True)
    weights = jnp.exp2((scores - row_max) * (LOG2E * float(HD) ** (-0.5)))
    denominator = jnp.sum(weights, axis=1, keepdims=True)
    return weights.astype(jnp.bfloat16), denominator


def blend(weights, denominator, values):
    blended = jnp.dot(weights, values, preferred_element_type=jnp.float32)
    return (blended / denominator).astype(jnp.bfloat16)


def attend(queries, keys, values, bias):
    weights, denominator = weigh(queries, keys, bias)
    return blend(weights, denominator, values)


def kernel(
    groups,
    features,
    qkv,
    mask,
    latent,
    w_head,
    step,
    dest,
    out,
    mask_held,
    latent_held,
    step_held,
    dest_held,
    small_sem,
    w_raw,
    w_own,
    w_sem,
    lat_rows,
    vel_rows,
    sh_q,
    sh_kv,
    own,
    held_weights,
    held_sums,
    bias,
    part,
    sib_part,
    red,
    blocks,
    pick,
    pick_out,
    sib_pick,
    send_sem,
    recv_sem,
    local_sem,
    pair_send,
    pair_recv,
    half_send,
    half_recv,
    red_send,
    red_recv,
    blk_send,
    blk_recv,
    swap_send,
    swap_recv,
):
    chips = groups // 2
    pairs = chips // 2
    rows = groups * BLK
    half = BLK // 2
    sect = lax.axis_index("sect")
    me = lax.axis_index("seq")
    chip = me // 2
    core = me % 2
    sibling = chip * 2 + 1 - core

    barrier = pltpu.get_barrier_semaphore()

    def greet_seq(k, _):
        peer = lax.rem(me + k, groups)
        pl.semaphore_signal(barrier, inc=1, device_id=(sect, peer), device_id_type=MESH)
        return 0

    def greet_sect(c, _):
        pl.semaphore_signal(
            barrier, inc=1, device_id=(1 - sect, (c * 2 + chip % 2) * 2 + core), device_id_type=MESH
        )
        return 0

    lax.fori_loop(1, groups, greet_seq, 0)
    lax.fori_loop(0, chips // 2, greet_sect, 0)
    pl.semaphore_wait(barrier, groups - 1 + chips // 2)

    def ends(stage, sender, target):
        t_chip = target // 2
        t_core = target % 2
        if stage < 2:
            columns = pl.ds(pl.multiple_of((t_chip * 5 + 4) * HD, HD), HD)
        else:
            columns = pl.ds(pl.multiple_of((t_chip * 5 + t_core * 2 + min(stage - 2, 1)) * HD, HD), HD)
        place = pl.ds(pl.multiple_of(sender * BLK, BLK), BLK)
        if stage == 0:
            src = qkv.at[0, 0, pl.ds(pl.multiple_of(t_core * half, half), half), columns]
            return src, sh_q.at[sender]
        if stage == 1:
            return qkv.at[0, 1 + t_core, :, columns], sh_kv.at[t_core, place, :]
        if stage == 2:
            return qkv.at[0, :, :, columns], own.at[0, :, place, :]
        if stage == 3:
            return qkv.at[0, pl.ds(0, 2), :, columns], own.at[1, pl.ds(0, 2), place, :]
        return qkv.at[0, 2, :, columns], own.at[1, 2, place, :]

    def remote(stage, sender, target):
        src, dst = ends(stage, sender, target)
        return pltpu.make_async_remote_copy(
            src_ref=src,
            dst_ref=dst,
            send_sem=send_sem.at[stage, target],
            recv_sem=recv_sem.at[stage, sender],
            device_id=(sect, target),
            device_id_type=MESH,
        )

    def local(stage):
        src, dst = ends(stage, me, me)
        return pltpu.make_async_copy(src, dst, local_sem.at[stage])

    def partner(bits):
        found = 0
        place = 1
        while place < groups:
            digit = me // place % 2
            found = found + place * ((1 - digit) if bits & place else digit)
            place *= 2
        return found

    for stages in ((1, 0), (2,), (3,), (4,)):
        for bits in range(1, groups):
            for stage in stages:
                remote(stage, me, partner(bits)).start()
        for stage in stages:
            local(stage).start()

    def arrive(stage):
        def one(k, _):
            sender = lax.rem(me + groups - k, groups)
            src, dst = ends(stage, sender, me)
            pltpu.make_async_remote_copy(
                src_ref=src,
                dst_ref=dst,
                send_sem=send_sem.at[stage, sender],
                recv_sem=recv_sem.at[stage, sender],
                device_id=(sect, sender),
                device_id_type=MESH,
            ).wait_recv()
            return 0

        lax.fori_loop(1, groups, one, 0)
        local(stage).wait()

    w_copies = []
    for slot, head in enumerate((4, core * 2, core * 2 + 1)):
        columns = pl.ds(pl.multiple_of((chip * 5 + head) * HD, HD), HD)
        w_copies.append(
            pltpu.make_async_copy(w_head.at[0, :, columns], w_raw.at[slot], w_sem.at[slot])
        )
        w_copies[-1].start()
    small_copies = [
        pltpu.make_async_copy(mask, mask_held, small_sem.at[0]),
        pltpu.make_async_copy(latent, latent_held, small_sem.at[1]),
        pltpu.make_async_copy(step, step_held, small_sem.at[2]),
        pltpu.make_async_copy(dest, dest_held, small_sem.at[3]),
    ]
    for small in small_copies:
        small.start()
    for small in small_copies:
        small.wait()
    for row in range(half):
        lat_rows[row : row + 1, :] = latent_held[0, :, row * BLK : (row + 1) * BLK]
    for slot in range(3):
        w_copies[slot].wait()
        turned = w_raw[slot]
        w_own[slot, 0] = jnp.concatenate([turned, jnp.zeros_like(turned)], axis=0)
        w_own[slot, 1] = jnp.concatenate([jnp.zeros_like(turned), turned], axis=0)

    expand = (
        lax.broadcasted_iota(jnp.int32, (groups, rows), 1) // BLK
        == lax.broadcasted_iota(jnp.int32, (groups, rows), 0)
    ).astype(jnp.float32)
    wide = jnp.dot(mask_held[0].astype(jnp.float32), expand, preferred_element_type=jnp.float32)
    bias[...] = jnp.where(wide > 0.5, 0.0, -jnp.inf).reshape(groups, 1, rows)

    def pair_copy(index, src, dst):
        return pltpu.make_async_remote_copy(
            src_ref=src,
            dst_ref=dst,
            send_sem=pair_send.at[index],
            recv_sem=pair_recv.at[index],
            device_id=(sect, sibling),
            device_id_type=MESH,
        )

    def contribute(slot, attended, block, first):
        across = (((1,), (1,)), ((), ()))
        product = lax.dot_general(
            attended[:half], w_own[slot, 0], across, preferred_element_type=jnp.float32
        ) + lax.dot_general(
            attended[half:], w_own[slot, 1], across, preferred_element_type=jnp.float32
        )
        wide_out = attended.astype(jnp.float32)
        squared = wide_out * wide_out
        upper = squared.astype(jnp.bfloat16)
        lower = (squared - upper.astype(jnp.float32)).astype(jnp.bfloat16)
        squares = lax.dot_general(
            jnp.ones((8, 2 * HD), jnp.bfloat16),
            jnp.concatenate([upper, lower], axis=1),
            (((1,), (1,)), ((), ())),
            preferred_element_type=jnp.float32,
        )
        both = jnp.concatenate([product, squares], axis=0)
        if first:
            part[block % 2, block // 2] = both
        else:
            part[block % 2, block // 2] += both

    arrive(1)
    handed = pair_copy(0, sh_kv.at[core], sh_kv.at[core])
    handed.start()
    arrive(0)
    pltpu.make_async_remote_copy(
        src_ref=sh_kv.at[1 - core],
        dst_ref=sh_kv.at[1 - core],
        send_sem=pair_send.at[0],
        recv_sem=pair_recv.at[0],
        device_id=(sect, sibling),
        device_id_type=MESH,
    ).wait_recv()

    def shared_step(turn, _):
        first = turn * SHARED_BLOCKS
        queries = sh_q[pl.ds(first, SHARED_BLOCKS)].reshape(SHARED_BLOCKS * half, HD)
        got = attend(queries, sh_kv[0], sh_kv[1], bias[pl.ds(first, SHARED_BLOCKS)])
        got = got.astype(jnp.float32)
        for index in range(SHARED_BLOCKS):
            piece = got[index * half : (index + 1) * half]
            zero = jnp.zeros_like(piece)
            low = jnp.where(core == 0, piece, zero)
            high = jnp.where(core == 0, zero, piece)
            attended = jnp.concatenate([low, high], axis=0).astype(jnp.bfloat16)
            contribute(0, attended, first + index, True)
        return 0

    lax.fori_loop(0, groups // SHARED_BLOCKS, shared_step, 0, unroll=UNROLL)

    for head in range(1):
        arrive(2 + head)

        def own_step(turn, _, head=head):
            first = turn * OWN_BLOCKS
            place = pl.ds(pl.multiple_of(first * BLK, BLK), OWN_BLOCKS * BLK)
            got = attend(
                own[head, 0, place, :], own[head, 1], own[head, 2], bias[pl.ds(first, OWN_BLOCKS)]
            )
            for index in range(OWN_BLOCKS):
                piece = got[index * BLK : (index + 1) * BLK]
                contribute(1 + head, piece, first + index, False)
            return 0

        lax.fori_loop(0, groups // OWN_BLOCKS, own_step, 0, unroll=UNROLL)

    def red_copy(source, target):
        return pltpu.make_async_remote_copy(
            src_ref=part.at[core, target],
            dst_ref=red.at[source],
            send_sem=red_send.at[target],
            recv_sem=red_recv.at[source],
            device_id=(sect, target * 2 + core),
            device_id_type=MESH,
        )

    def half_copy(target):
        return pltpu.make_async_remote_copy(
            src_ref=part.at[1 - core, target],
            dst_ref=sib_part.at[target],
            send_sem=half_send.at[target],
            recv_sem=half_recv.at[target],
            device_id=(sect, sibling),
            device_id_type=MESH,
        )

    def chip_partner(bits):
        found = 0
        place = 1
        while place < chips:
            digit = chip // place % 2
            flip = bits // place % 2
            found = found + place * (digit + flip - 2 * digit * flip)
            place *= 2
        return found

    arrive(3)

    def weigh_step(turn, _):
        first = turn * OWN_BLOCKS
        place = pl.ds(pl.multiple_of(first * BLK, BLK), OWN_BLOCKS * BLK)
        weights, denominator = weigh(own[1, 0, place, :], own[1, 1], bias[pl.ds(first, OWN_BLOCKS)])
        held_weights[place, :] = weights
        held_sums[place, :] = jnp.broadcast_to(denominator, (OWN_BLOCKS * BLK, HD))
        return 0

    lax.fori_loop(0, groups // OWN_BLOCKS, weigh_step, 0)
    arrive(4)

    def join(target):
        half_copy(target).wait_recv()
        part[core, target] += sib_part[target]

    def targets(step):
        turn = step % pairs
        return chip_partner(chips - 1 - 2 * turn), chip_partner(chips - 2 - 2 * turn)

    def settle(step):
        outer, inner = targets(step)
        join(outer)
        red_copy(chip, outer).start()

        @pl.when(step % pairs < pairs - 1)
        def _():
            join(inner)
            red_copy(chip, inner).start()

    def last_step(step, _):
        owner = step // pairs
        outer, inner = targets(step)
        places = [
            pl.ds(pl.multiple_of((target * 2 + owner) * BLK, BLK), BLK) for target in (outer, inner)
        ]
        weights = jnp.concatenate([held_weights[place, :] for place in places], axis=0)
        sums = jnp.concatenate([held_sums[place, :] for place in places], axis=0)
        blended = jnp.dot(weights, own[1, 2], preferred_element_type=jnp.float32)
        got = (blended / sums).astype(jnp.bfloat16)
        contribute(2, got[:BLK], outer * 2 + owner, False)
        contribute(2, got[BLK:], inner * 2 + owner, False)

        @pl.when(owner != core)
        def _():
            half_copy(outer).start()
            half_copy(inner).start()

        @pl.when(jnp.logical_and(step >= 1, (step - 1) // pairs == core))
        def _():
            settle(step - 1)

        return 0

    lax.fori_loop(0, 2 * pairs, last_step, 0)

    @pl.when(core == 1)
    def _():
        settle(2 * pairs - 1)

    join(chip)
    total = part[core, chip]
    for k in range(1, chips):
        source = lax.rem(chip + chips - k, chips)
        red_copy(source, source).wait_recv()
        total = total + red[source]

    levels = chips // 2
    level = chip // 2
    side = chip % 2
    member = me % 4
    scale_row = lax.rsqrt(total[half : half + 1] * (1.0 / features) + EPSILON)
    row_id = lax.broadcasted_iota(jnp.int32, (half, BLK), 0)
    lane_id = lax.broadcasted_iota(jnp.int32, (half, BLK), 1)
    scale_low = jnp.sum(jnp.where(lane_id == row_id, scale_row, 0.0), axis=1, keepdims=True)
    scale_high = jnp.sum(
        jnp.where(lane_id == row_id + half, scale_row, 0.0), axis=1, keepdims=True
    )
    scale = jnp.where(lane_id < half, scale_low, scale_high)
    vel_rows[...] = step_held[0] * (scale * total[:half])
    even = vel_rows[pl.ds(0, half // 2, stride=2), :]
    odd = vel_rows[pl.ds(1, half // 2, stride=2), :]
    upper_rows = jnp.concatenate([even[:, :half], odd[:, :half]], axis=1)
    lower_rows = jnp.concatenate([even[:, half:], odd[:, half:]], axis=1)
    updated = lat_rows[...] + jnp.concatenate([upper_rows, lower_rows], axis=0)
    blocks[sect, level] = updated.astype(jnp.bfloat16)

    def blk_copy(kind, from_sect, source, to_sect, target):
        return pltpu.make_async_remote_copy(
            src_ref=blocks.at[from_sect, source],
            dst_ref=blocks.at[from_sect, source],
            send_sem=blk_send.at[kind, target],
            recv_sem=blk_recv.at[kind, source],
            device_id=(to_sect, (target * 2 + side) * 2 + core),
            device_id_type=MESH,
        )

    @pl.when(sect == 0)
    def _():
        for k in range(levels):
            blk_copy(1, 0, level, 1, lax.rem(level + k, levels)).start()

    for k in range(1, levels):
        blk_copy(0, sect, level, sect, lax.rem(level + k, levels)).start()

    def choose(from_sect, source, block):
        named = jnp.full(block.shape, dest_held[from_sect * groups + source * 4 + member])
        for owner in range(4):
            for slot in range(CAP):
                number = (sect * groups + level * 4 + owner) * CAP + slot
                pick[owner, slot] += jnp.where(named == number, block, 0.0)

    pick[...] = jnp.zeros_like(pick)
    choose(sect, level, updated)
    for k in range(1, levels):
        source = lax.rem(level + levels - k, levels)
        blk_copy(0, sect, source, sect, source).wait_recv()
        choose(sect, source, blocks[sect, source].astype(jnp.float32))

    @pl.when(sect == 1)
    def _():
        for k in range(levels):
            source = lax.rem(level + levels - k, levels)
            blk_copy(1, 0, source, 1, source).wait_recv()
            choose(0, source, blocks[0, source].astype(jnp.float32))

    pick_out[...] = pick[...].astype(jnp.bfloat16)

    def swap(source, target):
        return pltpu.make_async_remote_copy(
            src_ref=pick_out.at[target],
            dst_ref=sib_pick.at[source],
            send_sem=swap_send.at[target],
            recv_sem=swap_recv.at[source],
            device_id=(sect, level * 4 + target),
            device_id_type=MESH,
        )

    for k in (2, 3, 1):
        swap(member, lax.rem(member + k, 4)).start()
    gathered = pick[member]
    for k in (1, 2, 3):
        source = lax.rem(member + 4 - k, 4)
        swap(source, source).wait_recv()
        gathered = gathered + sib_pick[source].astype(jnp.float32)
    for slot in range(CAP):
        placed = gathered[slot]
        for row in range(half):
            out[0, slot : slot + 1, row * BLK : (row + 1) * BLK] = placed[row : row + 1]

    half_copy(chip).wait_send()
    handed.wait_send()
    for k in range(1, 4):
        swap(member, lax.rem(member + k, 4)).wait_send()
    for k in range(1, chips):
        target = lax.rem(chip + k, chips)
        red_copy(chip, target).wait_send()
        half_copy(target).wait_send()
    for k in range(1, levels):
        blk_copy(0, sect, level, sect, lax.rem(level + k, levels)).wait_send()

    @pl.when(sect == 0)
    def _():
        for k in range(levels):
            blk_copy(1, 0, level, 1, lax.rem(level + k, levels)).wait_send()

    for stage in range(5):
        def sent(k, _, stage=stage):
            remote(stage, me, lax.rem(me + k, groups)).wait_send()
            return 0

        lax.fori_loop(1, groups, sent, 0)


def kernel_body(qkv, mask, latent, w_head, step, dest):
    groups = lax.axis_size("seq")
    features = qkv.shape[3]
    chips = groups // 2
    rows = groups * BLK
    half = BLK // 2
    channels = w_head.shape[2]
    turned = jnp.swapaxes(w_head, 1, 2)
    vmem = pl.BlockSpec(memory_space=pltpu.VMEM)
    hbm = pl.BlockSpec(memory_space=pl.ANY)
    dma = pltpu.SemaphoreType.DMA
    return pl.pallas_call(
        functools.partial(kernel, groups, features),
        out_shape=jax.ShapeDtypeStruct((1, CAP, latent.shape[2]), jnp.float32),
        in_specs=[hbm, hbm, hbm, hbm, pl.BlockSpec(memory_space=pltpu.HBM), hbm],
        out_specs=vmem,
        scratch_shapes=[
            pltpu.VMEM(mask.shape, jnp.int32),
            pltpu.VMEM(latent.shape, jnp.float32),
            pltpu.SMEM(step.shape, jnp.float32),
            pltpu.SMEM(dest.shape, jnp.int32),
            dma((4,)),
            pltpu.VMEM((3, channels, HD), jnp.bfloat16),
            pltpu.VMEM((3, 2, 2 * channels, HD), jnp.bfloat16),
            dma((3,)),
            pltpu.VMEM((half, BLK), jnp.float32),
            pltpu.VMEM((half, BLK), jnp.float32),
            pltpu.VMEM((groups, half, HD), jnp.bfloat16),
            pltpu.VMEM((2, rows, HD), jnp.bfloat16),
            pltpu.VMEM((2, 3, rows, HD), jnp.bfloat16),
            pltpu.VMEM((rows, rows), jnp.bfloat16),
            pltpu.VMEM((rows, HD), jnp.float32),
            pltpu.VMEM((groups, 1, rows), jnp.float32),
            pltpu.VMEM((2, chips, half + 8, BLK), jnp.float32),
            pltpu.VMEM((chips, half + 8, BLK), jnp.float32),
            pltpu.VMEM((chips, half + 8, BLK), jnp.float32),
            pltpu.VMEM((2, chips // 2, half, BLK), jnp.bfloat16),
            pltpu.VMEM((4, CAP, half, BLK), jnp.float32),
            pltpu.VMEM((4, CAP, half, BLK), jnp.bfloat16),
            pltpu.VMEM((4, CAP, half, BLK), jnp.bfloat16),
            dma((5, groups)),
            dma((5, groups)),
            dma((5,)),
            dma((1,)),
            dma((1,)),
            dma((chips,)),
            dma((chips,)),
            dma((chips,)),
            dma((chips,)),
            dma((2, chips // 2)),
            dma((2, chips // 2)),
            dma((4,)),
            dma((4,)),
        ],
        compiler_params=pltpu.CompilerParams(
            collective_id=0, has_side_effects=True, vmem_limit_bytes=61 * 1024 * 1024
        ),
    )(qkv, mask, latent, turned, step, dest)


def body(qkv, mask, latent, w_head, step, dest):
    groups = lax.axis_size("seq")
    heads = qkv.shape[3] // HD
    fits = (
        heads * 2 == groups * 5
        and qkv.shape[2] == BLK
        and latent.shape[1] == 1
        and w_head.shape[2] * 2 == BLK
        and lax.axis_size("sect") == 2
    )
    chosen = kernel_body if fits else general_body
    return chosen(qkv, mask, latent, w_head, step, dest)


def solution(mesh):
    in_specs = (
        P("sect", None, "seq", None),
        P("sect", None, None),
        P("sect", "seq", None),
        P("sect", None, None),
        P("sect"),
        P(),
    )
    out_specs = P("sect", "seq", None)
    return jax.shard_map(body, mesh=mesh, in_specs=in_specs, out_specs=out_specs, check_vma=False)
```

```python
import functools

import jax
import jax.numpy as jnp
from jax import lax
from jax.experimental import pallas as pl
from jax.experimental.pallas import tpu as pltpu
from jax.sharding import PartitionSpec as P

HD = 128
HG = 8
BLK = 128
CAP = 2


EPSILON = 1e-06


def general_body(qkv, mask, latent, w_head, step, dest):
    groups = lax.axis_size("seq")
    tok_rows = qkv.shape[2]
    features = qkv.shape[3]
    position = lax.axis_index("seq")
    block_count = mask.shape[1]
    score_scale = float(HD) ** (-0.5)
    row_groups = groups // HG
    group_width = features // HG
    per_piece = tok_rows // row_groups
    row_group = position % row_groups
    query_parts = qkv[0, 0].reshape(row_groups, per_piece, HG, group_width)
    pair_parts = qkv[0, 1:].reshape(2, tok_rows, HG, group_width).transpose(2, 0, 1, 3)
    query_send = query_parts.transpose(2, 0, 1, 3).reshape(groups, per_piece, group_width)
    pair_send = jnp.broadcast_to(pair_parts[:, None], (HG, row_groups, 2, tok_rows, group_width))
    pair_send = pair_send.reshape(groups, 2, tok_rows, group_width)
    arrived_query, arrived_pairs = (
        lax.all_to_all(query_send, "seq", split_axis=0, concat_axis=0, tiled=True),
        lax.all_to_all(pair_send, "seq", split_axis=0, concat_axis=0, tiled=True),
    )
    query_rows = arrived_query.reshape(groups * per_piece, group_width)
    key_rows = arrived_pairs[:, 0].reshape(groups * tok_rows, group_width)
    value_rows = arrived_pairs[:, 1].reshape(groups * tok_rows, group_width)
    query_count = groups * per_piece
    query_pos = jnp.arange(groups, dtype=jnp.int32)[:, None] * tok_rows + row_group * per_piece
    query_pos = (query_pos + jnp.arange(per_piece, dtype=jnp.int32)[None, :]).reshape(query_count)
    selector = (
        query_pos[:, None] // BLK == jnp.arange(block_count, dtype=jnp.int32)[None, :]
    ).astype(jnp.bfloat16)
    block_rows = jnp.dot(selector, mask[0].astype(jnp.bfloat16), preferred_element_type=jnp.float32)
    allowed = jnp.broadcast_to((block_rows > 0.5)[:, :, None], (query_count, block_count, BLK))
    allowed = allowed.reshape(query_count, block_count * BLK)
    outputs = []
    for head_index in range(group_width // HD):
        lower = head_index * HD
        scores = (
            jnp.einsum(
                "qd,kd->qk",
                query_rows[:, lower : lower + HD],
                key_rows[:, lower : lower + HD],
                preferred_element_type=jnp.float32,
            )
            * score_scale
        )
        scores = jnp.where(allowed, scores, -jnp.inf)
        row_max = jnp.max(scores, axis=1, keepdims=True)
        weights = jnp.exp(scores - row_max)
        denominator = jnp.sum(weights, axis=1, keepdims=True)
        blended = (
            jnp.dot(
                weights.astype(jnp.bfloat16),
                value_rows[:, lower : lower + HD],
                preferred_element_type=jnp.float32,
            )
            / denominator
        )
        outputs.append(blended.astype(jnp.bfloat16))
    attended = jnp.concatenate(outputs, axis=1)
    homeward = lax.all_to_all(
        attended.reshape(groups, per_piece, group_width),
        "seq",
        split_axis=0,
        concat_axis=0,
        tiled=True,
    )
    token_major = homeward.reshape(HG, row_groups, per_piece, group_width).transpose(1, 2, 0, 3)
    token_major = token_major.reshape(tok_rows, features)
    mean_square = jnp.mean(jnp.square(token_major.astype(jnp.float32)), axis=1)
    product = jnp.dot(token_major, w_head[0], preferred_element_type=jnp.float32)
    velocity = lax.rsqrt(mean_square + EPSILON)[:, None] * product
    updated = latent[0] + step[0] * velocity.reshape(latent.shape[1], latent.shape[2])
    sect_index = lax.axis_index("sect")
    device_rank = sect_index * groups + position
    owned_slots = device_rank * CAP + jnp.arange(CAP, dtype=jnp.int32)
    picker = (owned_slots[:, None] == dest[None, :]).astype(jnp.float32)
    placed = jnp.dot(
        picker,
        lax.all_gather(updated, ("sect", "seq"), axis=0, tiled=True),
        precision=lax.Precision.HIGHEST,
        preferred_element_type=jnp.float32,
    )
    return placed[None]


MESH = pl.DeviceIdType.MESH
LOG2E = 1.4426950408889634
SHARED_BLOCKS = 4
OWN_BLOCKS = 2
UNROLL = 1


def weigh(queries, keys, bias):
    scores = lax.dot_general(
        queries, keys, (((1,), (1,)), ((), ())), preferred_element_type=jnp.float32
    )
    count = bias.shape[0]
    keyed = scores.reshape(count, scores.shape[0] // count, scores.shape[1]) + bias
    scores = keyed.reshape(scores.shape)
    row_max = jnp.max(scores, axis=1, keepdims=True)
    weights = jnp.exp2((scores - row_max) * (LOG2E * float(HD) ** (-0.5)))
    denominator = jnp.sum(weights, axis=1, keepdims=True)
    return weights.astype(jnp.bfloat16), denominator


def blend(weights, denominator, values):
    blended = jnp.dot(weights, values, preferred_element_type=jnp.float32)
    return (blended / denominator).astype(jnp.bfloat16)


def attend(queries, keys, values, bias):
    weights, denominator = weigh(queries, keys, bias)
    return blend(weights, denominator, values)


def kernel(
    groups,
    features,
    qkv,
    mask,
    latent,
    w_head,
    step,
    dest,
    out,
    mask_held,
    latent_held,
    step_held,
    dest_held,
    small_sem,
    w_raw,
    w_own,
    w_sem,
    lat_rows,
    vel_rows,
    sh_q,
    sh_kv,
    own,
    held_weights,
    held_sums,
    bias,
    part,
    sib_part,
    red,
    blocks,
    pick,
    pick_out,
    sib_pick,
    send_sem,
    recv_sem,
    local_sem,
    pair_send,
    pair_recv,
    half_send,
    half_recv,
    red_send,
    red_recv,
    blk_send,
    blk_recv,
    swap_send,
    swap_recv,
):
    chips = groups // 2
    pairs = chips // 2
    rows = groups * BLK
    half = BLK // 2
    sect = lax.axis_index("sect")
    me = lax.axis_index("seq")
    chip = me // 2
    core = me % 2
    sibling = chip * 2 + 1 - core

    barrier = pltpu.get_barrier_semaphore()

    def greet_seq(k, _):
        peer = lax.rem(me + k, groups)
        pl.semaphore_signal(barrier, inc=1, device_id=(sect, peer), device_id_type=MESH)
        return 0

    def greet_sect(c, _):
        pl.semaphore_signal(
            barrier, inc=1, device_id=(1 - sect, (c * 2 + chip % 2) * 2 + core), device_id_type=MESH
        )
        return 0

    lax.fori_loop(1, groups, greet_seq, 0)
    lax.fori_loop(0, chips // 2, greet_sect, 0)
    pl.semaphore_wait(barrier, groups - 1 + chips // 2)

    def ends(stage, sender, target):
        t_chip = target // 2
        t_core = target % 2
        if stage < 2:
            columns = pl.ds(pl.multiple_of((t_chip * 5 + 4) * HD, HD), HD)
        else:
            head = stage % 2
            columns = pl.ds(pl.multiple_of((t_chip * 5 + t_core * 2 + head) * HD, HD), HD)
        place = pl.ds(pl.multiple_of(sender * BLK, BLK), BLK)
        if stage == 0:
            src = qkv.at[0, 0, pl.ds(pl.multiple_of(t_core * half, half), half), columns]
            return src, sh_q.at[sender]
        if stage == 1:
            return qkv.at[0, 1 + t_core, :, columns], sh_kv.at[t_core, place, :]
        if stage < 4:
            return qkv.at[0, pl.ds(0, 2), :, columns], own.at[head, pl.ds(0, 2), place, :]
        return qkv.at[0, 2, :, columns], own.at[head, 2, place, :]

    def remote(stage, sender, target):
        src, dst = ends(stage, sender, target)
        return pltpu.make_async_remote_copy(
            src_ref=src,
            dst_ref=dst,
            send_sem=send_sem.at[stage, target],
            recv_sem=recv_sem.at[stage, sender],
            device_id=(sect, target),
            device_id_type=MESH,
        )

    def local(stage):
        src, dst = ends(stage, me, me)
        return pltpu.make_async_copy(src, dst, local_sem.at[stage])

    def partner(bits):
        found = 0
        place = 1
        while place < groups:
            digit = me // place % 2
            found = found + place * ((1 - digit) if bits & place else digit)
            place *= 2
        return found

    for stages in ((1, 0), (2,), (3,), (4,), (5,)):
        for bits in range(1, groups):
            for stage in stages:
                remote(stage, me, partner(bits)).start()
        for stage in stages:
            local(stage).start()

    def all_sent(*stages):
        def sent(k, _):
            for stage in stages:
                remote(stage, me, lax.rem(me + k, groups)).wait_send()
            return 0

        lax.fori_loop(1, groups, sent, 0)

    def arrive(stage):
        def one(k, _):
            sender = lax.rem(me + groups - k, groups)
            src, dst = ends(stage, sender, me)
            pltpu.make_async_remote_copy(
                src_ref=src,
                dst_ref=dst,
                send_sem=send_sem.at[stage, sender],
                recv_sem=recv_sem.at[stage, sender],
                device_id=(sect, sender),
                device_id_type=MESH,
            ).wait_recv()
            return 0

        lax.fori_loop(1, groups, one, 0)
        local(stage).wait()

    w_copies = []
    for slot, head in enumerate((4, core * 2, core * 2 + 1)):
        columns = pl.ds(pl.multiple_of((chip * 5 + head) * HD, HD), HD)
        w_copies.append(
            pltpu.make_async_copy(w_head.at[0, :, columns], w_raw.at[slot], w_sem.at[slot])
        )
        w_copies[-1].start()
    small_copies = [
        pltpu.make_async_copy(mask, mask_held, small_sem.at[0]),
        pltpu.make_async_copy(latent, latent_held, small_sem.at[1]),
        pltpu.make_async_copy(step, step_held, small_sem.at[2]),
        pltpu.make_async_copy(dest, dest_held, small_sem.at[3]),
    ]
    for small in small_copies:
        small.start()
    for small in small_copies:
        small.wait()
    for row in range(half):
        lat_rows[row : row + 1, :] = latent_held[0, :, row * BLK : (row + 1) * BLK]
    for slot in range(3):
        w_copies[slot].wait()
        turned = w_raw[slot]
        w_own[slot, 0] = jnp.concatenate([turned, jnp.zeros_like(turned)], axis=0)
        w_own[slot, 1] = jnp.concatenate([jnp.zeros_like(turned), turned], axis=0)

    expand = (
        lax.broadcasted_iota(jnp.int32, (groups, rows), 1) // BLK
        == lax.broadcasted_iota(jnp.int32, (groups, rows), 0)
    ).astype(jnp.float32)
    wide = jnp.dot(mask_held[0].astype(jnp.float32), expand, preferred_element_type=jnp.float32)
    bias[...] = jnp.where(wide > 0.5, 0.0, -jnp.inf).reshape(groups, 1, rows)

    def pair_copy(index, src, dst):
        return pltpu.make_async_remote_copy(
            src_ref=src,
            dst_ref=dst,
            send_sem=pair_send.at[index],
            recv_sem=pair_recv.at[index],
            device_id=(sect, sibling),
            device_id_type=MESH,
        )

    def contribute(slot, attended, block, first):
        across = (((1,), (1,)), ((), ()))
        product = lax.dot_general(
            attended[:half], w_own[slot, 0], across, preferred_element_type=jnp.float32
        ) + lax.dot_general(
            attended[half:], w_own[slot, 1], across, preferred_element_type=jnp.float32
        )
        wide_out = attended.astype(jnp.float32)
        squared = wide_out * wide_out
        upper = squared.astype(jnp.bfloat16)
        lower = (squared - upper.astype(jnp.float32)).astype(jnp.bfloat16)
        squares = lax.dot_general(
            jnp.ones((8, 2 * HD), jnp.bfloat16),
            jnp.concatenate([upper, lower], axis=1),
            (((1,), (1,)), ((), ())),
            preferred_element_type=jnp.float32,
        )
        both = jnp.concatenate([product, squares], axis=0)
        if first:
            part[block % 2, block // 2] = both
        else:
            part[block % 2, block // 2] += both

    def contribute_all(slot, attended, blocks_named):
        count = len(blocks_named)
        pieces = attended.reshape(count, 2, half, HD)
        low = pieces[:, 0].reshape(count * half, HD)
        high = pieces[:, 1].reshape(count * half, HD)
        product = lax.dot_general(
            jnp.concatenate([low, high], axis=1),
            jnp.concatenate([w_own[slot, 0], w_own[slot, 1]], axis=1),
            (((1,), (1,)), ((), ())),
            preferred_element_type=jnp.float32,
        )
        wide_out = attended.astype(jnp.float32)
        squared = wide_out * wide_out
        upper = squared.astype(jnp.bfloat16)
        lower = (squared - upper.astype(jnp.float32)).astype(jnp.bfloat16)
        squares = lax.dot_general(
            jnp.ones((8, 2 * HD), jnp.bfloat16),
            jnp.concatenate([upper, lower], axis=1),
            (((1,), (1,)), ((), ())),
            preferred_element_type=jnp.float32,
        )
        for index, (owner, target) in enumerate(blocks_named):
            part[owner, target, :half] += product[index * half : (index + 1) * half]
            part[owner, target, half:] += squares[:, index * BLK : (index + 1) * BLK]

    arrive(1)
    handed = pair_copy(0, sh_kv.at[core], sh_kv.at[core])
    handed.start()
    arrive(0)
    pltpu.make_async_remote_copy(
        src_ref=sh_kv.at[1 - core],
        dst_ref=sh_kv.at[1 - core],
        send_sem=pair_send.at[0],
        recv_sem=pair_recv.at[0],
        device_id=(sect, sibling),
        device_id_type=MESH,
    ).wait_recv()

    def shared_step(turn, _):
        first = turn * SHARED_BLOCKS
        queries = sh_q[pl.ds(first, SHARED_BLOCKS)].reshape(SHARED_BLOCKS * half, HD)
        got = attend(queries, sh_kv[0], sh_kv[1], bias[pl.ds(first, SHARED_BLOCKS)])
        got = got.astype(jnp.float32)
        for index in range(SHARED_BLOCKS):
            piece = got[index * half : (index + 1) * half]
            zero = jnp.zeros_like(piece)
            low = jnp.where(core == 0, piece, zero)
            high = jnp.where(core == 0, zero, piece)
            attended = jnp.concatenate([low, high], axis=0).astype(jnp.bfloat16)
            contribute(0, attended, first + index, True)
        return 0

    lax.fori_loop(0, groups // SHARED_BLOCKS, shared_step, 0, unroll=UNROLL)

    def red_copy(source, target):
        return pltpu.make_async_remote_copy(
            src_ref=part.at[core, target],
            dst_ref=red.at[source],
            send_sem=red_send.at[target],
            recv_sem=red_recv.at[source],
            device_id=(sect, target * 2 + core),
            device_id_type=MESH,
        )

    def half_copy(target):
        return pltpu.make_async_remote_copy(
            src_ref=part.at[1 - core, target],
            dst_ref=sib_part.at[target],
            send_sem=half_send.at[target],
            recv_sem=half_recv.at[target],
            device_id=(sect, sibling),
            device_id_type=MESH,
        )

    def chip_partner(bits):
        found = 0
        place = 1
        while place < chips:
            digit = chip // place % 2
            flip = bits // place % 2
            found = found + place * (digit + flip - 2 * digit * flip)
            place *= 2
        return found

    for head in range(2):
        arrive(2 + head)

        def weigh_step(turn, _, head=head):
            first = turn * OWN_BLOCKS
            place = pl.ds(pl.multiple_of(first * BLK, BLK), OWN_BLOCKS * BLK)
            weights, denominator = weigh(
                own[head, 0, place, :], own[head, 1], bias[pl.ds(first, OWN_BLOCKS)]
            )
            held_weights[head, place, :] = weights
            held_sums[head, place, :] = jnp.broadcast_to(denominator, (OWN_BLOCKS * BLK, HD))
            return 0

        lax.fori_loop(0, groups // OWN_BLOCKS, weigh_step, 0)

    arrive(4)

    def own_step(turn, _):
        place = pl.ds(pl.multiple_of(turn * OWN_BLOCKS * BLK, BLK), OWN_BLOCKS * BLK)
        got = blend(held_weights[0, place, :], held_sums[0, place, :], own[0, 2])
        contribute_all(1, got, [(k % 2, turn * OWN_BLOCKS // 2 + k // 2) for k in range(OWN_BLOCKS)])
        return 0

    lax.fori_loop(0, groups // OWN_BLOCKS, own_step, 0)
    all_sent(0, 1, 2, 3)
    arrive(5)

    def join(target):
        half_copy(target).wait_recv()
        part[core, target] += sib_part[target]

    def targets(step):
        turn = step % pairs
        return chip_partner(chips - 1 - 2 * turn), chip_partner(chips - 2 - 2 * turn)

    def settle(step):
        outer, inner = targets(step)
        join(outer)
        red_copy(chip, outer).start()

        @pl.when(step % pairs < pairs - 1)
        def _():
            join(inner)
            red_copy(chip, inner).start()

    def last_step(step, _):
        owner = step // pairs
        outer, inner = targets(step)
        places = [
            pl.ds(pl.multiple_of((target * 2 + owner) * BLK, BLK), BLK) for target in (outer, inner)
        ]
        weights = jnp.concatenate([held_weights[1, place, :] for place in places], axis=0)
        sums = jnp.concatenate([held_sums[1, place, :] for place in places], axis=0)
        blended = jnp.dot(weights, own[1, 2], preferred_element_type=jnp.float32)
        got = (blended / sums).astype(jnp.bfloat16)
        contribute_all(2, got, [(owner, outer), (owner, inner)])

        @pl.when(owner != core)
        def _():
            half_copy(outer).start()
            half_copy(inner).start()

        @pl.when(jnp.logical_and(step >= 1, (step - 1) // pairs == core))
        def _():
            settle(step - 1)

        return 0

    lax.fori_loop(0, 2 * pairs, last_step, 0)

    @pl.when(core == 1)
    def _():
        settle(2 * pairs - 1)

    join(chip)
    all_sent(4, 5)
    handed.wait_send()
    total = part[core, chip]
    for k in range(1, chips):
        source = lax.rem(chip + chips - k, chips)
        red_copy(source, source).wait_recv()
        total = total + red[source]

    levels = chips // 2
    level = chip // 2
    side = chip % 2
    member = me % 4
    scale_row = lax.rsqrt(total[half : half + 1] * (1.0 / features) + EPSILON)
    row_id = lax.broadcasted_iota(jnp.int32, (half, BLK), 0)
    lane_id = lax.broadcasted_iota(jnp.int32, (half, BLK), 1)
    scale_low = jnp.sum(jnp.where(lane_id == row_id, scale_row, 0.0), axis=1, keepdims=True)
    scale_high = jnp.sum(
        jnp.where(lane_id == row_id + half, scale_row, 0.0), axis=1, keepdims=True
    )
    scale = jnp.where(lane_id < half, scale_low, scale_high)
    vel_rows[...] = step_held[0] * (scale * total[:half])
    even = vel_rows[pl.ds(0, half // 2, stride=2), :]
    odd = vel_rows[pl.ds(1, half // 2, stride=2), :]
    upper_rows = jnp.concatenate([even[:, :half], odd[:, :half]], axis=1)
    lower_rows = jnp.concatenate([even[:, half:], odd[:, half:]], axis=1)
    updated = lat_rows[...] + jnp.concatenate([upper_rows, lower_rows], axis=0)
    blocks[sect, level] = updated.astype(jnp.bfloat16)

    def blk_copy(kind, from_sect, source, to_sect, target):
        return pltpu.make_async_remote_copy(
            src_ref=blocks.at[from_sect, source],
            dst_ref=blocks.at[from_sect, source],
            send_sem=blk_send.at[kind, target],
            recv_sem=blk_recv.at[kind, source],
            device_id=(to_sect, (target * 2 + side) * 2 + core),
            device_id_type=MESH,
        )

    @pl.when(sect == 0)
    def _():
        for k in range(levels):
            blk_copy(1, 0, level, 1, lax.rem(level + k, levels)).start()

    for k in range(1, levels):
        blk_copy(0, sect, level, sect, lax.rem(level + k, levels)).start()

    def choose(from_sect, source, block):
        named = jnp.full(block.shape, dest_held[from_sect * groups + source * 4 + member])
        for owner in range(4):
            for slot in range(CAP):
                number = (sect * groups + level * 4 + owner) * CAP + slot
                pick[owner, slot] += jnp.where(named == number, block, 0.0)

    pick[...] = jnp.zeros_like(pick)
    choose(sect, level, updated)
    half_copy(chip).wait_send()
    for k in range(1, chips):
        target = lax.rem(chip + k, chips)
        red_copy(chip, target).wait_send()
        half_copy(target).wait_send()
    for k in range(1, levels):
        source = lax.rem(level + levels - k, levels)
        blk_copy(0, sect, source, sect, source).wait_recv()
        choose(sect, source, blocks[sect, source].astype(jnp.float32))

    @pl.when(sect == 1)
    def _():
        for k in range(levels):
            source = lax.rem(level + levels - k, levels)
            blk_copy(1, 0, source, 1, source).wait_recv()
            choose(0, source, blocks[0, source].astype(jnp.float32))

    pick_out[...] = pick[...].astype(jnp.bfloat16)

    def swap(source, target):
        return pltpu.make_async_remote_copy(
            src_ref=pick_out.at[target],
            dst_ref=sib_pick.at[source],
            send_sem=swap_send.at[target],
            recv_sem=swap_recv.at[source],
            device_id=(sect, level * 4 + target),
            device_id_type=MESH,
        )

    for k in (2, 3, 1):
        swap(member, lax.rem(member + k, 4)).start()
    gathered = pick[member]
    for k in (1, 2, 3):
        source = lax.rem(member + 4 - k, 4)
        swap(source, source).wait_recv()
        gathered = gathered + sib_pick[source].astype(jnp.float32)
    for slot in range(CAP):
        placed = gathered[slot]
        for row in range(half):
            out[0, slot : slot + 1, row * BLK : (row + 1) * BLK] = placed[row : row + 1]

    for k in range(1, 4):
        swap(member, lax.rem(member + k, 4)).wait_send()
    for k in range(1, levels):
        blk_copy(0, sect, level, sect, lax.rem(level + k, levels)).wait_send()

    @pl.when(sect == 0)
    def _():
        for k in range(levels):
            blk_copy(1, 0, level, 1, lax.rem(level + k, levels)).wait_send()


def kernel_body(qkv, mask, latent, w_head, step, dest):
    groups = lax.axis_size("seq")
    features = qkv.shape[3]
    chips = groups // 2
    rows = groups * BLK
    half = BLK // 2
    channels = w_head.shape[2]
    turned = jnp.swapaxes(w_head, 1, 2)
    vmem = pl.BlockSpec(memory_space=pltpu.VMEM)
    hbm = pl.BlockSpec(memory_space=pl.ANY)
    dma = pltpu.SemaphoreType.DMA
    return pl.pallas_call(
        functools.partial(kernel, groups, features),
        out_shape=jax.ShapeDtypeStruct((1, CAP, latent.shape[2]), jnp.float32),
        in_specs=[hbm, hbm, hbm, hbm, pl.BlockSpec(memory_space=pltpu.HBM), hbm],
        out_specs=vmem,
        scratch_shapes=[
            pltpu.VMEM(mask.shape, jnp.int32),
            pltpu.VMEM(latent.shape, jnp.float32),
            pltpu.SMEM(step.shape, jnp.float32),
            pltpu.SMEM(dest.shape, jnp.int32),
            dma((4,)),
            pltpu.VMEM((3, channels, HD), jnp.bfloat16),
            pltpu.VMEM((3, 2, 2 * channels, HD), jnp.bfloat16),
            dma((3,)),
            pltpu.VMEM((half, BLK), jnp.float32),
            pltpu.VMEM((half, BLK), jnp.float32),
            pltpu.VMEM((groups, half, HD), jnp.bfloat16),
            pltpu.VMEM((2, rows, HD), jnp.bfloat16),
            pltpu.VMEM((2, 3, rows, HD), jnp.bfloat16),
            pltpu.VMEM((2, rows, rows), jnp.bfloat16),
            pltpu.VMEM((2, rows, HD), jnp.float32),
            pltpu.VMEM((groups, 1, rows), jnp.float32),
            pltpu.VMEM((2, chips, half + 8, BLK), jnp.float32),
            pltpu.VMEM((chips, half + 8, BLK), jnp.float32),
            pltpu.VMEM((chips, half + 8, BLK), jnp.float32),
            pltpu.VMEM((2, chips // 2, half, BLK), jnp.bfloat16),
            pltpu.VMEM((4, CAP, half, BLK), jnp.float32),
            pltpu.VMEM((4, CAP, half, BLK), jnp.bfloat16),
            pltpu.VMEM((4, CAP, half, BLK), jnp.bfloat16),
            dma((6, groups)),
            dma((6, groups)),
            dma((6,)),
            dma((1,)),
            dma((1,)),
            dma((chips,)),
            dma((chips,)),
            dma((chips,)),
            dma((chips,)),
            dma((2, chips // 2)),
            dma((2, chips // 2)),
            dma((4,)),
            dma((4,)),
        ],
        compiler_params=pltpu.CompilerParams(
            collective_id=0, has_side_effects=True, vmem_limit_bytes=61 * 1024 * 1024
        ),
    )(qkv, mask, latent, turned, step, dest)


def body(qkv, mask, latent, w_head, step, dest):
    groups = lax.axis_size("seq")
    heads = qkv.shape[3] // HD
    fits = (
        heads * 2 == groups * 5
        and qkv.shape[2] == BLK
        and latent.shape[1] == 1
        and w_head.shape[2] * 2 == BLK
        and lax.axis_size("sect") == 2
    )
    chosen = kernel_body if fits else general_body
    return chosen(qkv, mask, latent, w_head, step, dest)


def solution(mesh):
    in_specs = (
        P("sect", None, "seq", None),
        P("sect", None, None),
        P("sect", "seq", None),
        P("sect", None, None),
        P("sect"),
        P(),
    )
    out_specs = P("sect", "seq", None)
    return jax.shard_map(body, mesh=mesh, in_specs=in_specs, out_specs=out_specs, check_vma=False)
```

```python
import functools

import jax
import jax.numpy as jnp
from jax import lax
from jax.experimental import pallas as pl
from jax.experimental.pallas import tpu as pltpu
from jax.sharding import PartitionSpec as P

HD = 128
HG = 8
BLK = 128
CAP = 2


EPSILON = 1e-06


def general_body(qkv, mask, latent, w_head, step, dest):
    groups = lax.axis_size("seq")
    tok_rows = qkv.shape[2]
    features = qkv.shape[3]
    position = lax.axis_index("seq")
    block_count = mask.shape[1]
    score_scale = float(HD) ** (-0.5)
    row_groups = groups // HG
    group_width = features // HG
    per_piece = tok_rows // row_groups
    row_group = position % row_groups
    query_parts = qkv[0, 0].reshape(row_groups, per_piece, HG, group_width)
    pair_parts = qkv[0, 1:].reshape(2, tok_rows, HG, group_width).transpose(2, 0, 1, 3)
    query_send = query_parts.transpose(2, 0, 1, 3).reshape(groups, per_piece, group_width)
    pair_send = jnp.broadcast_to(pair_parts[:, None], (HG, row_groups, 2, tok_rows, group_width))
    pair_send = pair_send.reshape(groups, 2, tok_rows, group_width)
    arrived_query, arrived_pairs = (
        lax.all_to_all(query_send, "seq", split_axis=0, concat_axis=0, tiled=True),
        lax.all_to_all(pair_send, "seq", split_axis=0, concat_axis=0, tiled=True),
    )
    query_rows = arrived_query.reshape(groups * per_piece, group_width)
    key_rows = arrived_pairs[:, 0].reshape(groups * tok_rows, group_width)
    value_rows = arrived_pairs[:, 1].reshape(groups * tok_rows, group_width)
    query_count = groups * per_piece
    query_pos = jnp.arange(groups, dtype=jnp.int32)[:, None] * tok_rows + row_group * per_piece
    query_pos = (query_pos + jnp.arange(per_piece, dtype=jnp.int32)[None, :]).reshape(query_count)
    selector = (
        query_pos[:, None] // BLK == jnp.arange(block_count, dtype=jnp.int32)[None, :]
    ).astype(jnp.bfloat16)
    block_rows = jnp.dot(selector, mask[0].astype(jnp.bfloat16), preferred_element_type=jnp.float32)
    allowed = jnp.broadcast_to((block_rows > 0.5)[:, :, None], (query_count, block_count, BLK))
    allowed = allowed.reshape(query_count, block_count * BLK)
    outputs = []
    for head_index in range(group_width // HD):
        lower = head_index * HD
        scores = (
            jnp.einsum(
                "qd,kd->qk",
                query_rows[:, lower : lower + HD],
                key_rows[:, lower : lower + HD],
                preferred_element_type=jnp.float32,
            )
            * score_scale
        )
        scores = jnp.where(allowed, scores, -jnp.inf)
        row_max = jnp.max(scores, axis=1, keepdims=True)
        weights = jnp.exp(scores - row_max)
        denominator = jnp.sum(weights, axis=1, keepdims=True)
        blended = (
            jnp.dot(
                weights.astype(jnp.bfloat16),
                value_rows[:, lower : lower + HD],
                preferred_element_type=jnp.float32,
            )
            / denominator
        )
        outputs.append(blended.astype(jnp.bfloat16))
    attended = jnp.concatenate(outputs, axis=1)
    homeward = lax.all_to_all(
        attended.reshape(groups, per_piece, group_width),
        "seq",
        split_axis=0,
        concat_axis=0,
        tiled=True,
    )
    token_major = homeward.reshape(HG, row_groups, per_piece, group_width).transpose(1, 2, 0, 3)
    token_major = token_major.reshape(tok_rows, features)
    mean_square = jnp.mean(jnp.square(token_major.astype(jnp.float32)), axis=1)
    product = jnp.dot(token_major, w_head[0], preferred_element_type=jnp.float32)
    velocity = lax.rsqrt(mean_square + EPSILON)[:, None] * product
    updated = latent[0] + step[0] * velocity.reshape(latent.shape[1], latent.shape[2])
    sect_index = lax.axis_index("sect")
    device_rank = sect_index * groups + position
    owned_slots = device_rank * CAP + jnp.arange(CAP, dtype=jnp.int32)
    picker = (owned_slots[:, None] == dest[None, :]).astype(jnp.float32)
    placed = jnp.dot(
        picker,
        lax.all_gather(updated, ("sect", "seq"), axis=0, tiled=True),
        precision=lax.Precision.HIGHEST,
        preferred_element_type=jnp.float32,
    )
    return placed[None]


MESH = pl.DeviceIdType.MESH
LOG2E = 1.4426950408889634
SHARED_BLOCKS = 4
OWN_BLOCKS = 4
UNROLL = 1
LAG = 2


def weigh(queries, keys, bias):
    scores = lax.dot_general(
        queries, keys, (((1,), (1,)), ((), ())), preferred_element_type=jnp.float32
    )
    count = bias.shape[0]
    keyed = scores.reshape(count, scores.shape[0] // count, scores.shape[1]) + bias
    scores = keyed.reshape(scores.shape)
    row_max = jnp.max(scores, axis=1, keepdims=True)
    weights = jnp.exp2((scores - row_max) * (LOG2E * float(HD) ** (-0.5)))
    denominator = jnp.sum(weights, axis=1, keepdims=True)
    return weights.astype(jnp.bfloat16), denominator


def blend(weights, denominator, values):
    blended = jnp.dot(weights, values, preferred_element_type=jnp.float32)
    return (blended / denominator).astype(jnp.bfloat16)


def attend(queries, keys, values, bias):
    weights, denominator = weigh(queries, keys, bias)
    return blend(weights, denominator, values)


def kernel(
    groups,
    features,
    qkv,
    mask,
    latent,
    w_head,
    step,
    dest,
    out,
    mask_held,
    latent_held,
    step_held,
    dest_held,
    small_sem,
    w_raw,
    w_own,
    w_sem,
    lat_rows,
    vel_rows,
    sh_q,
    sh_kv,
    own,
    held_weights,
    held_sums,
    bias,
    part,
    sib_part,
    red,
    blocks,
    pick,
    pick_out,
    sib_pick,
    send_sem,
    recv_sem,
    local_sem,
    pair_send,
    pair_recv,
    half_send,
    half_recv,
    red_send,
    red_recv,
    blk_send,
    blk_recv,
    swap_send,
    swap_recv,
):
    chips = groups // 2
    pairs = chips // 2
    rows = groups * BLK
    half = BLK // 2
    sect = lax.axis_index("sect")
    me = lax.axis_index("seq")
    chip = me // 2
    core = me % 2
    sibling = chip * 2 + 1 - core

    barrier = pltpu.get_barrier_semaphore()

    def greet_seq(k, _):
        peer = lax.rem(me + chips + k, groups)
        pl.semaphore_signal(barrier, inc=1, device_id=(sect, peer), device_id_type=MESH)
        return 0

    def greet_sect(c, _):
        pl.semaphore_signal(
            barrier, inc=1, device_id=(1 - sect, (c * 2 + chip % 2) * 2 + core), device_id_type=MESH
        )
        return 0

    lax.fori_loop(0, chips, greet_seq, 0)
    lax.fori_loop(chips + 1, groups, greet_seq, 0)
    lax.fori_loop(0, chips // 2, greet_sect, 0)
    pl.semaphore_wait(barrier, groups - 1 + chips // 2)

    def ends(stage, sender, target):
        t_chip = target // 2
        t_core = target % 2
        if stage < 2:
            columns = pl.ds(pl.multiple_of((t_chip * 5 + 4) * HD, HD), HD)
        else:
            head = stage % 2
            columns = pl.ds(pl.multiple_of((t_chip * 5 + t_core * 2 + head) * HD, HD), HD)
        place = pl.ds(pl.multiple_of(sender * BLK, BLK), BLK)
        if stage == 0:
            src = qkv.at[0, 0, pl.ds(pl.multiple_of(t_core * half, half), half), columns]
            return src, sh_q.at[sender]
        if stage == 1:
            return qkv.at[0, 1 + t_core, :, columns], sh_kv.at[t_core, place, :]
        if stage < 4:
            return qkv.at[0, pl.ds(0, 2), :, columns], own.at[head, pl.ds(0, 2), place, :]
        return qkv.at[0, 2, :, columns], own.at[head, 2, place, :]

    def remote(stage, sender, target):
        src, dst = ends(stage, sender, target)
        return pltpu.make_async_remote_copy(
            src_ref=src,
            dst_ref=dst,
            send_sem=send_sem.at[stage, target],
            recv_sem=recv_sem.at[stage, sender],
            device_id=(sect, target),
            device_id_type=MESH,
        )

    def local(stage):
        src, dst = ends(stage, me, me)
        return pltpu.make_async_copy(src, dst, local_sem.at[stage])

    def partner(bits):
        found = 0
        place = 1
        while place < groups:
            digit = me // place % 2
            found = found + place * ((1 - digit) if bits & place else digit)
            place *= 2
        return found

    for stages in ((1, 0), (2,), (3,), (4,), (5,)):
        for bits in range(1, groups):
            for stage in stages:
                remote(stage, me, partner(bits)).start()
        for stage in stages:
            local(stage).start()

    def all_sent(*stages):
        def sent(k, _):
            for stage in stages:
                remote(stage, me, lax.rem(me + k, groups)).wait_send()
            return 0

        lax.fori_loop(1, groups, sent, 0)

    def arrive(stage):
        def one(k, _):
            sender = lax.rem(me + groups - k, groups)
            src, dst = ends(stage, sender, me)
            pltpu.make_async_remote_copy(
                src_ref=src,
                dst_ref=dst,
                send_sem=send_sem.at[stage, sender],
                recv_sem=recv_sem.at[stage, sender],
                device_id=(sect, sender),
                device_id_type=MESH,
            ).wait_recv()
            return 0

        lax.fori_loop(1, groups, one, 0)
        local(stage).wait()

    w_copies = []
    for slot, head in enumerate((4, core * 2, core * 2 + 1)):
        columns = pl.ds(pl.multiple_of((chip * 5 + head) * HD, HD), HD)
        w_copies.append(
            pltpu.make_async_copy(w_head.at[0, :, columns], w_raw.at[slot], w_sem.at[slot])
        )
        w_copies[-1].start()
    small_copies = [
        pltpu.make_async_copy(mask, mask_held, small_sem.at[0]),
        pltpu.make_async_copy(latent, latent_held, small_sem.at[1]),
        pltpu.make_async_copy(step, step_held, small_sem.at[2]),
        pltpu.make_async_copy(dest, dest_held, small_sem.at[3]),
    ]
    for small in small_copies:
        small.start()
    for small in small_copies:
        small.wait()
    for row in range(half):
        lat_rows[row : row + 1, :] = latent_held[0, :, row * BLK : (row + 1) * BLK]
    for slot in range(3):
        w_copies[slot].wait()
        turned = w_raw[slot]
        w_own[slot, 0] = jnp.concatenate([turned, jnp.zeros_like(turned)], axis=0)
        w_own[slot, 1] = jnp.concatenate([jnp.zeros_like(turned), turned], axis=0)

    expand = (
        lax.broadcasted_iota(jnp.int32, (groups, rows), 1) // BLK
        == lax.broadcasted_iota(jnp.int32, (groups, rows), 0)
    ).astype(jnp.float32)
    wide = jnp.dot(mask_held[0].astype(jnp.float32), expand, preferred_element_type=jnp.float32)
    bias[...] = jnp.where(wide > 0.5, 0.0, -jnp.inf).reshape(groups, 1, rows)

    def pair_copy(index, src, dst):
        return pltpu.make_async_remote_copy(
            src_ref=src,
            dst_ref=dst,
            send_sem=pair_send.at[index],
            recv_sem=pair_recv.at[index],
            device_id=(sect, sibling),
            device_id_type=MESH,
        )

    def contribute(slot, attended, block, first):
        across = (((1,), (1,)), ((), ()))
        product = lax.dot_general(
            attended[:half], w_own[slot, 0], across, preferred_element_type=jnp.float32
        ) + lax.dot_general(
            attended[half:], w_own[slot, 1], across, preferred_element_type=jnp.float32
        )
        wide_out = attended.astype(jnp.float32)
        squared = wide_out * wide_out
        upper = squared.astype(jnp.bfloat16)
        lower = (squared - upper.astype(jnp.float32)).astype(jnp.bfloat16)
        squares = lax.dot_general(
            jnp.ones((8, 2 * HD), jnp.bfloat16),
            jnp.concatenate([upper, lower], axis=1),
            (((1,), (1,)), ((), ())),
            preferred_element_type=jnp.float32,
        )
        both = jnp.concatenate([product, squares], axis=0)
        if first:
            part[block % 2, block // 2] = both
        else:
            part[block % 2, block // 2] += both

    def contribute_all(slot, attended, blocks_named):
        count = len(blocks_named)
        pieces = attended.reshape(count, 2, half, HD)
        low = pieces[:, 0].reshape(count * half, HD)
        high = pieces[:, 1].reshape(count * half, HD)
        product = lax.dot_general(
            jnp.concatenate([low, high], axis=1),
            jnp.concatenate([w_own[slot, 0], w_own[slot, 1]], axis=1),
            (((1,), (1,)), ((), ())),
            preferred_element_type=jnp.float32,
        )
        wide_out = attended.astype(jnp.float32)
        squared = wide_out * wide_out
        upper = squared.astype(jnp.bfloat16)
        lower = (squared - upper.astype(jnp.float32)).astype(jnp.bfloat16)
        squares = lax.dot_general(
            jnp.ones((8, 2 * HD), jnp.bfloat16),
            jnp.concatenate([upper, lower], axis=1),
            (((1,), (1,)), ((), ())),
            preferred_element_type=jnp.float32,
        )
        for index, (owner, target) in enumerate(blocks_named):
            part[owner, target, :half] += product[index * half : (index + 1) * half]
            part[owner, target, half:] += squares[:, index * BLK : (index + 1) * BLK]

    arrive(1)
    handed = pair_copy(0, sh_kv.at[core], sh_kv.at[core])
    handed.start()
    arrive(0)
    pltpu.make_async_remote_copy(
        src_ref=sh_kv.at[1 - core],
        dst_ref=sh_kv.at[1 - core],
        send_sem=pair_send.at[0],
        recv_sem=pair_recv.at[0],
        device_id=(sect, sibling),
        device_id_type=MESH,
    ).wait_recv()

    def shared_step(turn, _):
        first = turn * SHARED_BLOCKS
        queries = sh_q[pl.ds(first, SHARED_BLOCKS)].reshape(SHARED_BLOCKS * half, HD)
        got = attend(queries, sh_kv[0], sh_kv[1], bias[pl.ds(first, SHARED_BLOCKS)])
        got = got.astype(jnp.float32)
        for index in range(SHARED_BLOCKS):
            piece = got[index * half : (index + 1) * half]
            zero = jnp.zeros_like(piece)
            low = jnp.where(core == 0, piece, zero)
            high = jnp.where(core == 0, zero, piece)
            attended = jnp.concatenate([low, high], axis=0).astype(jnp.bfloat16)
            contribute(0, attended, first + index, True)
        return 0

    lax.fori_loop(0, groups // SHARED_BLOCKS, shared_step, 0, unroll=UNROLL)

    def red_copy(source, target):
        return pltpu.make_async_remote_copy(
            src_ref=part.at[core, target],
            dst_ref=red.at[source],
            send_sem=red_send.at[target],
            recv_sem=red_recv.at[source],
            device_id=(sect, target * 2 + core),
            device_id_type=MESH,
        )

    def half_copy(target):
        return pltpu.make_async_remote_copy(
            src_ref=part.at[1 - core, target],
            dst_ref=sib_part.at[target],
            send_sem=half_send.at[target],
            recv_sem=half_recv.at[target],
            device_id=(sect, sibling),
            device_id_type=MESH,
        )

    def chip_partner(bits):
        found = 0
        place = 1
        while place < chips:
            digit = chip // place % 2
            flip = bits // place % 2
            found = found + place * (digit + flip - 2 * digit * flip)
            place *= 2
        return found

    for head in range(2):
        arrive(2 + head)

        def weigh_step(turn, _, head=head):
            first = turn * OWN_BLOCKS
            place = pl.ds(pl.multiple_of(first * BLK, BLK), OWN_BLOCKS * BLK)
            weights, denominator = weigh(
                own[head, 0, place, :], own[head, 1], bias[pl.ds(first, OWN_BLOCKS)]
            )
            held_weights[head, place, :] = weights
            held_sums[head, place, :] = jnp.broadcast_to(denominator, (OWN_BLOCKS * BLK, HD))
            return 0

        lax.fori_loop(0, groups // OWN_BLOCKS, weigh_step, 0)

    arrive(4)

    def own_step(turn, _):
        place = pl.ds(pl.multiple_of(turn * OWN_BLOCKS * BLK, BLK), OWN_BLOCKS * BLK)
        got = blend(held_weights[0, place, :], held_sums[0, place, :], own[0, 2])
        contribute_all(1, got, [(k % 2, turn * OWN_BLOCKS // 2 + k // 2) for k in range(OWN_BLOCKS)])
        return 0

    lax.fori_loop(0, groups // OWN_BLOCKS, own_step, 0)
    all_sent(0, 1, 2, 3)
    arrive(5)

    def join(target):
        half_copy(target).wait_recv()
        part[core, target] += sib_part[target]

    def targets(step):
        turn = step % pairs
        return chip_partner(chips - 1 - 2 * turn), chip_partner(chips - 2 - 2 * turn)

    def settle(step):
        outer, inner = targets(step)
        join(outer)
        red_copy(chip, outer).start()

        @pl.when(step % pairs < pairs - 1)
        def _():
            join(inner)
            red_copy(chip, inner).start()

    def last_step(step, _):
        owner = step // pairs
        outer, inner = targets(step)
        places = [
            pl.ds(pl.multiple_of((target * 2 + owner) * BLK, BLK), BLK) for target in (outer, inner)
        ]
        weights = jnp.concatenate([held_weights[1, place, :] for place in places], axis=0)
        sums = jnp.concatenate([held_sums[1, place, :] for place in places], axis=0)
        blended = jnp.dot(weights, own[1, 2], preferred_element_type=jnp.float32)
        got = (blended / sums).astype(jnp.bfloat16)
        contribute_all(2, got, [(owner, outer), (owner, inner)])

        @pl.when(owner != core)
        def _():
            half_copy(outer).start()
            half_copy(inner).start()

        @pl.when(jnp.logical_and(step >= LAG, (step - LAG) // pairs == core))
        def _():
            settle(step - LAG)

        return 0

    lax.fori_loop(0, 2 * pairs, last_step, 0)

    @pl.when(core == 1)
    def _():
        for step in range(2 * pairs - LAG, 2 * pairs):
            settle(step)

    join(chip)
    all_sent(4, 5)
    handed.wait_send()
    total = part[core, chip]
    for k in range(1, chips):
        source = lax.rem(chip + chips - k, chips)
        red_copy(source, source).wait_recv()
        total = total + red[source]

    levels = chips // 2
    level = chip // 2
    side = chip % 2
    member = me % 4
    scale_row = lax.rsqrt(total[half : half + 1] * (1.0 / features) + EPSILON)
    row_id = lax.broadcasted_iota(jnp.int32, (half, BLK), 0)
    lane_id = lax.broadcasted_iota(jnp.int32, (half, BLK), 1)
    scale_low = jnp.sum(jnp.where(lane_id == row_id, scale_row, 0.0), axis=1, keepdims=True)
    scale_high = jnp.sum(
        jnp.where(lane_id == row_id + half, scale_row, 0.0), axis=1, keepdims=True
    )
    scale = jnp.where(lane_id < half, scale_low, scale_high)
    vel_rows[...] = step_held[0] * (scale * total[:half])
    even = vel_rows[pl.ds(0, half // 2, stride=2), :]
    odd = vel_rows[pl.ds(1, half // 2, stride=2), :]
    upper_rows = jnp.concatenate([even[:, :half], odd[:, :half]], axis=1)
    lower_rows = jnp.concatenate([even[:, half:], odd[:, half:]], axis=1)
    updated = lat_rows[...] + jnp.concatenate([upper_rows, lower_rows], axis=0)
    blocks[sect, level] = updated.astype(jnp.bfloat16)

    def blk_copy(kind, from_sect, source, to_sect, target):
        return pltpu.make_async_remote_copy(
            src_ref=blocks.at[from_sect, source],
            dst_ref=blocks.at[from_sect, source],
            send_sem=blk_send.at[kind, target],
            recv_sem=blk_recv.at[kind, source],
            device_id=(to_sect, (target * 2 + side) * 2 + core),
            device_id_type=MESH,
        )

    @pl.when(sect == 0)
    def _():
        for k in range(levels):
            blk_copy(1, 0, level, 1, lax.rem(level + k, levels)).start()

    for k in range(1, levels):
        blk_copy(0, sect, level, sect, lax.rem(level + k, levels)).start()

    def choose(from_sect, source, block):
        named = jnp.full(block.shape, dest_held[from_sect * groups + source * 4 + member])
        for owner in range(4):
            for slot in range(CAP):
                number = (sect * groups + level * 4 + owner) * CAP + slot
                pick[owner, slot] += jnp.where(named == number, block, 0.0)

    pick[...] = jnp.zeros_like(pick)
    choose(sect, level, updated)
    half_copy(chip).wait_send()
    for k in range(1, chips):
        target = lax.rem(chip + k, chips)
        red_copy(chip, target).wait_send()
        half_copy(target).wait_send()
    for k in range(1, levels):
        source = lax.rem(level + levels - k, levels)
        blk_copy(0, sect, source, sect, source).wait_recv()
        choose(sect, source, blocks[sect, source].astype(jnp.float32))

    @pl.when(sect == 1)
    def _():
        for k in range(levels):
            source = lax.rem(level + levels - k, levels)
            blk_copy(1, 0, source, 1, source).wait_recv()
            choose(0, source, blocks[0, source].astype(jnp.float32))

    pick_out[...] = pick[...].astype(jnp.bfloat16)

    def swap(source, target):
        return pltpu.make_async_remote_copy(
            src_ref=pick_out.at[target],
            dst_ref=sib_pick.at[source],
            send_sem=swap_send.at[target],
            recv_sem=swap_recv.at[source],
            device_id=(sect, level * 4 + target),
            device_id_type=MESH,
        )

    for k in (2, 3, 1):
        swap(member, lax.rem(member + k, 4)).start()
    gathered = pick[member]
    for k in (1, 2, 3):
        source = lax.rem(member + 4 - k, 4)
        swap(source, source).wait_recv()
        gathered = gathered + sib_pick[source].astype(jnp.float32)
    for slot in range(CAP):
        placed = gathered[slot]
        for row in range(half):
            out[0, slot : slot + 1, row * BLK : (row + 1) * BLK] = placed[row : row + 1]

    for k in range(1, 4):
        swap(member, lax.rem(member + k, 4)).wait_send()
    for k in range(1, levels):
        blk_copy(0, sect, level, sect, lax.rem(level + k, levels)).wait_send()

    @pl.when(sect == 0)
    def _():
        for k in range(levels):
            blk_copy(1, 0, level, 1, lax.rem(level + k, levels)).wait_send()


def kernel_body(qkv, mask, latent, w_head, step, dest):
    groups = lax.axis_size("seq")
    features = qkv.shape[3]
    chips = groups // 2
    rows = groups * BLK
    half = BLK // 2
    channels = w_head.shape[2]
    turned = jnp.swapaxes(w_head, 1, 2)
    vmem = pl.BlockSpec(memory_space=pltpu.VMEM)
    hbm = pl.BlockSpec(memory_space=pl.ANY)
    dma = pltpu.SemaphoreType.DMA
    return pl.pallas_call(
        functools.partial(kernel, groups, features),
        out_shape=jax.ShapeDtypeStruct((1, CAP, latent.shape[2]), jnp.float32),
        in_specs=[hbm, hbm, hbm, hbm, pl.BlockSpec(memory_space=pltpu.HBM), hbm],
        out_specs=vmem,
        scratch_shapes=[
            pltpu.VMEM(mask.shape, jnp.int32),
            pltpu.VMEM(latent.shape, jnp.float32),
            pltpu.SMEM(step.shape, jnp.float32),
            pltpu.SMEM(dest.shape, jnp.int32),
            dma((4,)),
            pltpu.VMEM((3, channels, HD), jnp.bfloat16),
            pltpu.VMEM((3, 2, 2 * channels, HD), jnp.bfloat16),
            dma((3,)),
            pltpu.VMEM((half, BLK), jnp.float32),
            pltpu.VMEM((half, BLK), jnp.float32),
            pltpu.VMEM((groups, half, HD), jnp.bfloat16),
            pltpu.VMEM((2, rows, HD), jnp.bfloat16),
            pltpu.VMEM((2, 3, rows, HD), jnp.bfloat16),
            pltpu.VMEM((2, rows, rows), jnp.bfloat16),
            pltpu.VMEM((2, rows, HD), jnp.float32),
            pltpu.VMEM((groups, 1, rows), jnp.float32),
            pltpu.VMEM((2, chips, half + 8, BLK), jnp.float32),
            pltpu.VMEM((chips, half + 8, BLK), jnp.float32),
            pltpu.VMEM((chips, half + 8, BLK), jnp.float32),
            pltpu.VMEM((2, chips // 2, half, BLK), jnp.bfloat16),
            pltpu.VMEM((4, CAP, half, BLK), jnp.float32),
            pltpu.VMEM((4, CAP, half, BLK), jnp.bfloat16),
            pltpu.VMEM((4, CAP, half, BLK), jnp.bfloat16),
            dma((6, groups)),
            dma((6, groups)),
            dma((6,)),
            dma((1,)),
            dma((1,)),
            dma((chips,)),
            dma((chips,)),
            dma((chips,)),
            dma((chips,)),
            dma((2, chips // 2)),
            dma((2, chips // 2)),
            dma((4,)),
            dma((4,)),
        ],
        compiler_params=pltpu.CompilerParams(
            collective_id=0, has_side_effects=True, vmem_limit_bytes=61 * 1024 * 1024
        ),
    )(qkv, mask, latent, turned, step, dest)


def body(qkv, mask, latent, w_head, step, dest):
    groups = lax.axis_size("seq")
    heads = qkv.shape[3] // HD
    fits = (
        heads * 2 == groups * 5
        and qkv.shape[2] == BLK
        and latent.shape[1] == 1
        and w_head.shape[2] * 2 == BLK
        and lax.axis_size("sect") == 2
    )
    chosen = kernel_body if fits else general_body
    return chosen(qkv, mask, latent, w_head, step, dest)


def solution(mesh):
    in_specs = (
        P("sect", None, "seq", None),
        P("sect", None, None),
        P("sect", "seq", None),
        P("sect", None, None),
        P("sect"),
        P(),
    )
    out_specs = P("sect", "seq", None)
    return jax.shard_map(body, mesh=mesh, in_specs=in_specs, out_specs=out_specs, check_vma=False)
```

```python
import functools

import jax
import jax.numpy as jnp
from jax import lax
from jax.experimental import pallas as pl
from jax.experimental.pallas import tpu as pltpu
from jax.sharding import PartitionSpec as P

HD = 128
HG = 8
BLK = 128
CAP = 2


EPSILON = 1e-06


def general_body(qkv, mask, latent, w_head, step, dest):
    groups = lax.axis_size("seq")
    tok_rows = qkv.shape[2]
    features = qkv.shape[3]
    position = lax.axis_index("seq")
    block_count = mask.shape[1]
    score_scale = float(HD) ** (-0.5)
    row_groups = groups // HG
    group_width = features // HG
    per_piece = tok_rows // row_groups
    row_group = position % row_groups
    query_parts = qkv[0, 0].reshape(row_groups, per_piece, HG, group_width)
    pair_parts = qkv[0, 1:].reshape(2, tok_rows, HG, group_width).transpose(2, 0, 1, 3)
    query_send = query_parts.transpose(2, 0, 1, 3).reshape(groups, per_piece, group_width)
    pair_send = jnp.broadcast_to(pair_parts[:, None], (HG, row_groups, 2, tok_rows, group_width))
    pair_send = pair_send.reshape(groups, 2, tok_rows, group_width)
    arrived_query, arrived_pairs = (
        lax.all_to_all(query_send, "seq", split_axis=0, concat_axis=0, tiled=True),
        lax.all_to_all(pair_send, "seq", split_axis=0, concat_axis=0, tiled=True),
    )
    query_rows = arrived_query.reshape(groups * per_piece, group_width)
    key_rows = arrived_pairs[:, 0].reshape(groups * tok_rows, group_width)
    value_rows = arrived_pairs[:, 1].reshape(groups * tok_rows, group_width)
    query_count = groups * per_piece
    query_pos = jnp.arange(groups, dtype=jnp.int32)[:, None] * tok_rows + row_group * per_piece
    query_pos = (query_pos + jnp.arange(per_piece, dtype=jnp.int32)[None, :]).reshape(query_count)
    selector = (
        query_pos[:, None] // BLK == jnp.arange(block_count, dtype=jnp.int32)[None, :]
    ).astype(jnp.bfloat16)
    block_rows = jnp.dot(selector, mask[0].astype(jnp.bfloat16), preferred_element_type=jnp.float32)
    allowed = jnp.broadcast_to((block_rows > 0.5)[:, :, None], (query_count, block_count, BLK))
    allowed = allowed.reshape(query_count, block_count * BLK)
    outputs = []
    for head_index in range(group_width // HD):
        lower = head_index * HD
        scores = (
            jnp.einsum(
                "qd,kd->qk",
                query_rows[:, lower : lower + HD],
                key_rows[:, lower : lower + HD],
                preferred_element_type=jnp.float32,
            )
            * score_scale
        )
        scores = jnp.where(allowed, scores, -jnp.inf)
        row_max = jnp.max(scores, axis=1, keepdims=True)
        weights = jnp.exp(scores - row_max)
        denominator = jnp.sum(weights, axis=1, keepdims=True)
        blended = (
            jnp.dot(
                weights.astype(jnp.bfloat16),
                value_rows[:, lower : lower + HD],
                preferred_element_type=jnp.float32,
            )
            / denominator
        )
        outputs.append(blended.astype(jnp.bfloat16))
    attended = jnp.concatenate(outputs, axis=1)
    homeward = lax.all_to_all(
        attended.reshape(groups, per_piece, group_width),
        "seq",
        split_axis=0,
        concat_axis=0,
        tiled=True,
    )
    token_major = homeward.reshape(HG, row_groups, per_piece, group_width).transpose(1, 2, 0, 3)
    token_major = token_major.reshape(tok_rows, features)
    mean_square = jnp.mean(jnp.square(token_major.astype(jnp.float32)), axis=1)
    product = jnp.dot(token_major, w_head[0], preferred_element_type=jnp.float32)
    velocity = lax.rsqrt(mean_square + EPSILON)[:, None] * product
    updated = latent[0] + step[0] * velocity.reshape(latent.shape[1], latent.shape[2])
    sect_index = lax.axis_index("sect")
    device_rank = sect_index * groups + position
    owned_slots = device_rank * CAP + jnp.arange(CAP, dtype=jnp.int32)
    picker = (owned_slots[:, None] == dest[None, :]).astype(jnp.float32)
    placed = jnp.dot(
        picker,
        lax.all_gather(updated, ("sect", "seq"), axis=0, tiled=True),
        precision=lax.Precision.HIGHEST,
        preferred_element_type=jnp.float32,
    )
    return placed[None]


MESH = pl.DeviceIdType.MESH
LOG2E = 1.4426950408889634
SHARED_BLOCKS = 4
OWN_BLOCKS = 4
UNROLL = 1
LAG = 2


def weigh(queries, keys, bias):
    scores = lax.dot_general(
        queries, keys, (((1,), (1,)), ((), ())), preferred_element_type=jnp.float32
    )
    count = bias.shape[0]
    keyed = scores.reshape(count, scores.shape[0] // count, scores.shape[1]) + bias
    scores = keyed.reshape(scores.shape)
    row_max = jnp.max(scores, axis=1, keepdims=True)
    weights = jnp.exp2((scores - row_max) * (LOG2E * float(HD) ** (-0.5)))
    denominator = jnp.sum(weights, axis=1, keepdims=True)
    return weights.astype(jnp.bfloat16), denominator


def blend(weights, denominator, values):
    blended = jnp.dot(weights, values, preferred_element_type=jnp.float32)
    return (blended / denominator).astype(jnp.bfloat16)


def attend(queries, keys, values, bias):
    weights, denominator = weigh(queries, keys, bias)
    return blend(weights, denominator, values)


def kernel(
    groups,
    features,
    qkv,
    mask,
    latent,
    w_head,
    step,
    dest,
    out,
    mask_held,
    latent_held,
    step_held,
    dest_held,
    small_sem,
    w_raw,
    w_own,
    w_sem,
    lat_rows,
    vel_rows,
    sh_q,
    sh_kv,
    own,
    held_weights,
    held_sums,
    bias,
    part,
    sib_part,
    red,
    blocks,
    pick,
    pick_out,
    sib_pick,
    send_sem,
    recv_sem,
    local_sem,
    pair_send,
    pair_recv,
    half_send,
    half_recv,
    red_send,
    red_recv,
    blk_send,
    blk_recv,
    swap_send,
    swap_recv,
):
    chips = groups // 2
    pairs = chips // 2
    rows = groups * BLK
    half = BLK // 2
    sect = lax.axis_index("sect")
    me = lax.axis_index("seq")
    chip = me // 2
    core = me % 2
    sibling = chip * 2 + 1 - core

    barrier = pltpu.get_barrier_semaphore()

    def greet_seq(k, _):
        peer = lax.rem(me + chips + k, groups)
        pl.semaphore_signal(barrier, inc=1, device_id=(sect, peer), device_id_type=MESH)
        return 0

    def greet_sect(c, _):
        pl.semaphore_signal(
            barrier, inc=1, device_id=(1 - sect, (c * 2 + chip % 2) * 2 + core), device_id_type=MESH
        )
        return 0

    lax.fori_loop(0, chips, greet_seq, 0)
    lax.fori_loop(chips + 1, groups, greet_seq, 0)
    lax.fori_loop(0, chips // 2, greet_sect, 0)
    pl.semaphore_wait(barrier, groups - 1 + chips // 2)

    def ends(stage, sender, target):
        t_chip = target // 2
        t_core = target % 2
        if stage < 2:
            columns = pl.ds(pl.multiple_of((t_chip * 5 + 4) * HD, HD), HD)
        else:
            head = stage % 2
            columns = pl.ds(pl.multiple_of((t_chip * 5 + t_core * 2 + head) * HD, HD), HD)
        place = pl.ds(pl.multiple_of(sender * BLK, BLK), BLK)
        if stage == 0:
            src = qkv.at[0, 0, pl.ds(pl.multiple_of(t_core * half, half), half), columns]
            return src, sh_q.at[sender]
        if stage == 1:
            return qkv.at[0, 1 + t_core, :, columns], sh_kv.at[t_core, place, :]
        if stage < 4:
            return qkv.at[0, pl.ds(0, 2), :, columns], own.at[head, pl.ds(0, 2), place, :]
        return qkv.at[0, 2, :, columns], own.at[head, 2, place, :]

    def remote(stage, sender, target):
        src, dst = ends(stage, sender, target)
        return pltpu.make_async_remote_copy(
            src_ref=src,
            dst_ref=dst,
            send_sem=send_sem.at[stage, target],
            recv_sem=recv_sem.at[stage, sender],
            device_id=(sect, target),
            device_id_type=MESH,
        )

    def local(stage):
        src, dst = ends(stage, me, me)
        return pltpu.make_async_copy(src, dst, local_sem.at[stage])

    def partner(bits):
        found = 0
        place = 1
        while place < groups:
            digit = me // place % 2
            found = found + place * ((1 - digit) if bits & place else digit)
            place *= 2
        return found

    def send_out(*stages):
        for bits in range(1, groups):
            for stage in stages:
                remote(stage, me, partner(bits)).start()
        for stage in stages:
            local(stage).start()

    send_out(1, 0)
    send_out(2)
    send_out(3)

    def all_sent(*stages):
        def sent(k, _):
            for stage in stages:
                remote(stage, me, lax.rem(me + k, groups)).wait_send()
            return 0

        lax.fori_loop(1, groups, sent, 0)

    def arrive(stage):
        def one(k, _):
            sender = lax.rem(me + groups - k, groups)
            src, dst = ends(stage, sender, me)
            pltpu.make_async_remote_copy(
                src_ref=src,
                dst_ref=dst,
                send_sem=send_sem.at[stage, sender],
                recv_sem=recv_sem.at[stage, sender],
                device_id=(sect, sender),
                device_id_type=MESH,
            ).wait_recv()
            return 0

        lax.fori_loop(1, groups, one, 0)
        local(stage).wait()

    w_copies = []
    for slot, head in enumerate((4, core * 2, core * 2 + 1)):
        columns = pl.ds(pl.multiple_of((chip * 5 + head) * HD, HD), HD)
        w_copies.append(
            pltpu.make_async_copy(w_head.at[0, :, columns], w_raw.at[slot], w_sem.at[slot])
        )
        w_copies[-1].start()
    small_copies = [
        pltpu.make_async_copy(mask, mask_held, small_sem.at[0]),
        pltpu.make_async_copy(latent, latent_held, small_sem.at[1]),
        pltpu.make_async_copy(step, step_held, small_sem.at[2]),
        pltpu.make_async_copy(dest, dest_held, small_sem.at[3]),
    ]
    for small in small_copies:
        small.start()
    for small in small_copies:
        small.wait()
    for row in range(half):
        lat_rows[row : row + 1, :] = latent_held[0, :, row * BLK : (row + 1) * BLK]
    for slot in range(3):
        w_copies[slot].wait()
        turned = w_raw[slot]
        w_own[slot, 0] = jnp.concatenate([turned, jnp.zeros_like(turned)], axis=0)
        w_own[slot, 1] = jnp.concatenate([jnp.zeros_like(turned), turned], axis=0)

    expand = (
        lax.broadcasted_iota(jnp.int32, (groups, rows), 1) // BLK
        == lax.broadcasted_iota(jnp.int32, (groups, rows), 0)
    ).astype(jnp.float32)
    wide = jnp.dot(mask_held[0].astype(jnp.float32), expand, preferred_element_type=jnp.float32)
    bias[...] = jnp.where(wide > 0.5, 0.0, -jnp.inf).reshape(groups, 1, rows)

    def pair_copy(index, src, dst):
        return pltpu.make_async_remote_copy(
            src_ref=src,
            dst_ref=dst,
            send_sem=pair_send.at[index],
            recv_sem=pair_recv.at[index],
            device_id=(sect, sibling),
            device_id_type=MESH,
        )

    def contribute(slot, attended, block, first):
        across = (((1,), (1,)), ((), ()))
        product = lax.dot_general(
            attended[:half], w_own[slot, 0], across, preferred_element_type=jnp.float32
        ) + lax.dot_general(
            attended[half:], w_own[slot, 1], across, preferred_element_type=jnp.float32
        )
        wide_out = attended.astype(jnp.float32)
        squared = wide_out * wide_out
        upper = squared.astype(jnp.bfloat16)
        lower = (squared - upper.astype(jnp.float32)).astype(jnp.bfloat16)
        squares = lax.dot_general(
            jnp.ones((8, 2 * HD), jnp.bfloat16),
            jnp.concatenate([upper, lower], axis=1),
            (((1,), (1,)), ((), ())),
            preferred_element_type=jnp.float32,
        )
        both = jnp.concatenate([product, squares], axis=0)
        if first:
            part[block % 2, block // 2] = both
        else:
            part[block % 2, block // 2] += both

    def contribute_all(slot, attended, blocks_named):
        count = len(blocks_named)
        pieces = attended.reshape(count, 2, half, HD)
        low = pieces[:, 0].reshape(count * half, HD)
        high = pieces[:, 1].reshape(count * half, HD)
        product = lax.dot_general(
            jnp.concatenate([low, high], axis=1),
            jnp.concatenate([w_own[slot, 0], w_own[slot, 1]], axis=1),
            (((1,), (1,)), ((), ())),
            preferred_element_type=jnp.float32,
        )
        wide_out = attended.astype(jnp.float32)
        squared = wide_out * wide_out
        upper = squared.astype(jnp.bfloat16)
        lower = (squared - upper.astype(jnp.float32)).astype(jnp.bfloat16)
        squares = lax.dot_general(
            jnp.ones((8, 2 * HD), jnp.bfloat16),
            jnp.concatenate([upper, lower], axis=1),
            (((1,), (1,)), ((), ())),
            preferred_element_type=jnp.float32,
        )
        for index, (owner, target) in enumerate(blocks_named):
            part[owner, target, :half] += product[index * half : (index + 1) * half]
            part[owner, target, half:] += squares[:, index * BLK : (index + 1) * BLK]

    arrive(1)
    handed = pair_copy(0, sh_kv.at[core], sh_kv.at[core])
    handed.start()
    arrive(0)
    pltpu.make_async_remote_copy(
        src_ref=sh_kv.at[1 - core],
        dst_ref=sh_kv.at[1 - core],
        send_sem=pair_send.at[0],
        recv_sem=pair_recv.at[0],
        device_id=(sect, sibling),
        device_id_type=MESH,
    ).wait_recv()

    def shared_step(turn, _):
        first = turn * SHARED_BLOCKS
        queries = sh_q[pl.ds(first, SHARED_BLOCKS)].reshape(SHARED_BLOCKS * half, HD)
        got = attend(queries, sh_kv[0], sh_kv[1], bias[pl.ds(first, SHARED_BLOCKS)])
        got = got.astype(jnp.float32)
        for index in range(SHARED_BLOCKS):
            piece = got[index * half : (index + 1) * half]
            zero = jnp.zeros_like(piece)
            low = jnp.where(core == 0, piece, zero)
            high = jnp.where(core == 0, zero, piece)
            attended = jnp.concatenate([low, high], axis=0).astype(jnp.bfloat16)
            contribute(0, attended, first + index, True)
        return 0

    lax.fori_loop(0, groups // SHARED_BLOCKS, shared_step, 0, unroll=UNROLL)

    def red_copy(source, target):
        return pltpu.make_async_remote_copy(
            src_ref=part.at[core, target],
            dst_ref=red.at[source],
            send_sem=red_send.at[target],
            recv_sem=red_recv.at[source],
            device_id=(sect, target * 2 + core),
            device_id_type=MESH,
        )

    def half_copy(target):
        return pltpu.make_async_remote_copy(
            src_ref=part.at[1 - core, target],
            dst_ref=sib_part.at[target],
            send_sem=half_send.at[target],
            recv_sem=half_recv.at[target],
            device_id=(sect, sibling),
            device_id_type=MESH,
        )

    def chip_partner(bits):
        found = 0
        place = 1
        while place < chips:
            digit = chip // place % 2
            flip = bits // place % 2
            found = found + place * (digit + flip - 2 * digit * flip)
            place *= 2
        return found

    for head in range(2):
        arrive(2 + head)
        if head == 0:
            send_out(4)
            send_out(5)

        def weigh_step(turn, _, head=head):
            first = turn * OWN_BLOCKS
            place = pl.ds(pl.multiple_of(first * BLK, BLK), OWN_BLOCKS * BLK)
            weights, denominator = weigh(
                own[head, 0, place, :], own[head, 1], bias[pl.ds(first, OWN_BLOCKS)]
            )
            held_weights[head, place, :] = weights
            held_sums[head, place, :] = jnp.broadcast_to(denominator, (OWN_BLOCKS * BLK, HD))
            return 0

        lax.fori_loop(0, groups // OWN_BLOCKS, weigh_step, 0)

    arrive(4)

    def own_step(turn, _):
        place = pl.ds(pl.multiple_of(turn * OWN_BLOCKS * BLK, BLK), OWN_BLOCKS * BLK)
        got = blend(held_weights[0, place, :], held_sums[0, place, :], own[0, 2])
        contribute_all(1, got, [(k % 2, turn * OWN_BLOCKS // 2 + k // 2) for k in range(OWN_BLOCKS)])
        return 0

    lax.fori_loop(0, groups // OWN_BLOCKS, own_step, 0)
    all_sent(0, 1, 2, 3)
    arrive(5)

    def join(target):
        half_copy(target).wait_recv()
        part[core, target] += sib_part[target]

    def targets(step):
        turn = step % pairs
        return chip_partner(chips - 1 - 2 * turn), chip_partner(chips - 2 - 2 * turn)

    def settle(step):
        outer, inner = targets(step)
        join(outer)
        red_copy(chip, outer).start()

        @pl.when(step % pairs < pairs - 1)
        def _():
            join(inner)
            red_copy(chip, inner).start()

    def last_step(step, _):
        owner = step // pairs
        outer, inner = targets(step)
        places = [
            pl.ds(pl.multiple_of((target * 2 + owner) * BLK, BLK), BLK) for target in (outer, inner)
        ]
        weights = jnp.concatenate([held_weights[1, place, :] for place in places], axis=0)
        sums = jnp.concatenate([held_sums[1, place, :] for place in places], axis=0)
        blended = jnp.dot(weights, own[1, 2], preferred_element_type=jnp.float32)
        got = (blended / sums).astype(jnp.bfloat16)
        contribute_all(2, got, [(owner, outer), (owner, inner)])

        @pl.when(owner != core)
        def _():
            half_copy(outer).start()
            half_copy(inner).start()

        @pl.when(jnp.logical_and(step >= LAG, (step - LAG) // pairs == core))
        def _():
            settle(step - LAG)

        return 0

    lax.fori_loop(0, 2 * pairs, last_step, 0)

    @pl.when(core == 1)
    def _():
        for step in range(2 * pairs - LAG, 2 * pairs):
            settle(step)

    join(chip)
    all_sent(4, 5)
    handed.wait_send()
    total = part[core, chip]
    for k in range(1, chips):
        source = lax.rem(chip + chips - k, chips)
        red_copy(source, source).wait_recv()
        total = total + red[source]

    levels = chips // 2
    level = chip // 2
    side = chip % 2
    member = me % 4
    scale_row = lax.rsqrt(total[half : half + 1] * (1.0 / features) + EPSILON)
    row_id = lax.broadcasted_iota(jnp.int32, (half, BLK), 0)
    lane_id = lax.broadcasted_iota(jnp.int32, (half, BLK), 1)
    scale_low = jnp.sum(jnp.where(lane_id == row_id, scale_row, 0.0), axis=1, keepdims=True)
    scale_high = jnp.sum(
        jnp.where(lane_id == row_id + half, scale_row, 0.0), axis=1, keepdims=True
    )
    scale = jnp.where(lane_id < half, scale_low, scale_high)
    vel_rows[...] = step_held[0] * (scale * total[:half])
    even = vel_rows[pl.ds(0, half // 2, stride=2), :]
    odd = vel_rows[pl.ds(1, half // 2, stride=2), :]
    upper_rows = jnp.concatenate([even[:, :half], odd[:, :half]], axis=1)
    lower_rows = jnp.concatenate([even[:, half:], odd[:, half:]], axis=1)
    updated = lat_rows[...] + jnp.concatenate([upper_rows, lower_rows], axis=0)
    blocks[sect, level] = updated.astype(jnp.bfloat16)

    def blk_copy(kind, from_sect, source, to_sect, target):
        return pltpu.make_async_remote_copy(
            src_ref=blocks.at[from_sect, source],
            dst_ref=blocks.at[from_sect, source],
            send_sem=blk_send.at[kind, target],
            recv_sem=blk_recv.at[kind, source],
            device_id=(to_sect, (target * 2 + side) * 2 + core),
            device_id_type=MESH,
        )

    @pl.when(sect == 0)
    def _():
        for k in range(levels):
            blk_copy(1, 0, level, 1, lax.rem(level + k, levels)).start()

    for k in range(1, levels):
        blk_copy(0, sect, level, sect, lax.rem(level + k, levels)).start()

    def choose(from_sect, source, block):
        named = jnp.full(block.shape, dest_held[from_sect * groups + source * 4 + member])
        for owner in range(4):
            for slot in range(CAP):
                number = (sect * groups + level * 4 + owner) * CAP + slot
                pick[owner, slot] += jnp.where(named == number, block, 0.0)

    pick[...] = jnp.zeros_like(pick)
    choose(sect, level, updated)
    half_copy(chip).wait_send()
    for k in range(1, chips):
        target = lax.rem(chip + k, chips)
        red_copy(chip, target).wait_send()
        half_copy(target).wait_send()
    for k in range(1, levels):
        source = lax.rem(level + levels - k, levels)
        blk_copy(0, sect, source, sect, source).wait_recv()
        choose(sect, source, blocks[sect, source].astype(jnp.float32))

    @pl.when(sect == 1)
    def _():
        for k in range(levels):
            source = lax.rem(level + levels - k, levels)
            blk_copy(1, 0, source, 1, source).wait_recv()
            choose(0, source, blocks[0, source].astype(jnp.float32))

    pick_out[...] = pick[...].astype(jnp.bfloat16)

    def swap(source, target):
        return pltpu.make_async_remote_copy(
            src_ref=pick_out.at[target],
            dst_ref=sib_pick.at[source],
            send_sem=swap_send.at[target],
            recv_sem=swap_recv.at[source],
            device_id=(sect, level * 4 + target),
            device_id_type=MESH,
        )

    for k in (2, 3, 1):
        swap(member, lax.rem(member + k, 4)).start()
    gathered = pick[member]
    for k in (1, 2, 3):
        source = lax.rem(member + 4 - k, 4)
        swap(source, source).wait_recv()
        gathered = gathered + sib_pick[source].astype(jnp.float32)
    for slot in range(CAP):
        placed = gathered[slot]
        for row in range(half):
            out[0, slot : slot + 1, row * BLK : (row + 1) * BLK] = placed[row : row + 1]

    for k in range(1, 4):
        swap(member, lax.rem(member + k, 4)).wait_send()
    for k in range(1, levels):
        blk_copy(0, sect, level, sect, lax.rem(level + k, levels)).wait_send()

    @pl.when(sect == 0)
    def _():
        for k in range(levels):
            blk_copy(1, 0, level, 1, lax.rem(level + k, levels)).wait_send()


def kernel_body(qkv, mask, latent, w_head, step, dest):
    groups = lax.axis_size("seq")
    features = qkv.shape[3]
    chips = groups // 2
    rows = groups * BLK
    half = BLK // 2
    channels = w_head.shape[2]
    turned = jnp.swapaxes(w_head, 1, 2)
    vmem = pl.BlockSpec(memory_space=pltpu.VMEM)
    hbm = pl.BlockSpec(memory_space=pl.ANY)
    dma = pltpu.SemaphoreType.DMA
    return pl.pallas_call(
        functools.partial(kernel, groups, features),
        out_shape=jax.ShapeDtypeStruct((1, CAP, latent.shape[2]), jnp.float32),
        in_specs=[hbm, hbm, hbm, hbm, pl.BlockSpec(memory_space=pltpu.HBM), hbm],
        out_specs=vmem,
        scratch_shapes=[
            pltpu.VMEM(mask.shape, jnp.int32),
            pltpu.VMEM(latent.shape, jnp.float32),
            pltpu.SMEM(step.shape, jnp.float32),
            pltpu.SMEM(dest.shape, jnp.int32),
            dma((4,)),
            pltpu.VMEM((3, channels, HD), jnp.bfloat16),
            pltpu.VMEM((3, 2, 2 * channels, HD), jnp.bfloat16),
            dma((3,)),
            pltpu.VMEM((half, BLK), jnp.float32),
            pltpu.VMEM((half, BLK), jnp.float32),
            pltpu.VMEM((groups, half, HD), jnp.bfloat16),
            pltpu.VMEM((2, rows, HD), jnp.bfloat16),
            pltpu.VMEM((2, 3, rows, HD), jnp.bfloat16),
            pltpu.VMEM((2, rows, rows), jnp.bfloat16),
            pltpu.VMEM((2, rows, HD), jnp.float32),
            pltpu.VMEM((groups, 1, rows), jnp.float32),
            pltpu.VMEM((2, chips, half + 8, BLK), jnp.float32),
            pltpu.VMEM((chips, half + 8, BLK), jnp.float32),
            pltpu.VMEM((chips, half + 8, BLK), jnp.float32),
            pltpu.VMEM((2, chips // 2, half, BLK), jnp.bfloat16),
            pltpu.VMEM((4, CAP, half, BLK), jnp.float32),
            pltpu.VMEM((4, CAP, half, BLK), jnp.bfloat16),
            pltpu.VMEM((4, CAP, half, BLK), jnp.bfloat16),
            dma((6, groups)),
            dma((6, groups)),
            dma((6,)),
            dma((1,)),
            dma((1,)),
            dma((chips,)),
            dma((chips,)),
            dma((chips,)),
            dma((chips,)),
            dma((2, chips // 2)),
            dma((2, chips // 2)),
            dma((4,)),
            dma((4,)),
        ],
        compiler_params=pltpu.CompilerParams(
            collective_id=0, has_side_effects=True, vmem_limit_bytes=61 * 1024 * 1024
        ),
    )(qkv, mask, latent, turned, step, dest)


def body(qkv, mask, latent, w_head, step, dest):
    groups = lax.axis_size("seq")
    heads = qkv.shape[3] // HD
    fits = (
        heads * 2 == groups * 5
        and qkv.shape[2] == BLK
        and latent.shape[1] == 1
        and w_head.shape[2] * 2 == BLK
        and lax.axis_size("sect") == 2
    )
    chosen = kernel_body if fits else general_body
    return chosen(qkv, mask, latent, w_head, step, dest)


def solution(mesh):
    in_specs = (
        P("sect", None, "seq", None),
        P("sect", None, None),
        P("sect", "seq", None),
        P("sect", None, None),
        P("sect"),
        P(),
    )
    out_specs = P("sect", "seq", None)
    return jax.shard_map(body, mesh=mesh, in_specs=in_specs, out_specs=out_specs, check_vma=False)
```
